768 devices in a mesh: dp: 4 (over x), expert: 48 (over z, y_lo), tensor: 4 (over y_hi, core).
Axes of the slice: x: 4, y: 8 (y_hi: 2, y_lo: 4; y = y_hi * 4 + y_lo), z: 12, core: 2. Of those that a mesh axis runs over, the one named last changes fastest.
Arguments:
- grad_out: bfloat16 [24576, 4096], P(('dp', 'expert')), may hold values from -6 to 6
- expert_ids: int32 [24576, 8], P(('dp', 'expert')), may hold values from 0 to 127, all different within a row
- gate_values: bfloat16 [24576, 8], P(('dp', 'expert')), may hold values from 0.019897461 to 0.5
- saved_hidden: bfloat16 [4, 48, 192, 1536], P('dp', 'expert', None, 'tensor'), may hold values from -0.59765625 to 0.59765625
- down_weight: bfloat16 [48, 1536, 4096], P('expert', 'tensor'), may hold values from -0.15625 to 0.15625
Outputs:
- gate_grad: float32 [24576, 8], P(('dp', 'expert'))
- hidden_grad: bfloat16 [4, 48, 192, 1536], P('dp', 'expert', None, 'tensor')
- down_grad: float32 [48, 1536, 4096], P('expert', 'tensor', 'dp')
The draws below stay inside these ranges and needn't reach their ends.
Inputs may be any that keep to these rules, and one draw needn't show every extreme that they name: `expert_ids`: the 8 experts of a row differ.
All inputs are finite; a program needn't handle non-finite values.
Results may differ from the reference program's by a relative error of at most 0.0085.
Values may be sent and summed in bfloat16 or wider, within the bound.
A program may use at most 32 MiB of HBM per device.

```python
import math
from functools import partial
import jax
import jax.numpy as jnp
from jax import lax

D = 4096
EXPERTS = 128
TOP = 8
FF = 1536
CAP = 4
TOK = 128
TOKENS = 24576
SLOTS = 192
N_DP = 4
N_EXPERT = 48


def block_scale(key, shape, shards, low, high):
    def one(position, shards_of):
        draws = jax.random.uniform(jax.random.fold_in(jax.random.fold_in(key, 6), position), (shards_of,), jnp.float32, low / len(shards), high / len(shards))
        return jnp.repeat(jnp.exp(draws), shape[position] // shards_of).reshape((-1,) + (1,) * (len(shape) - position - 1))

    loudness = one(*shards[0])
    for cut in shards[1:]:
        loudness = loudness * one(*cut)
    return loudness


def picks_of(stream_key, rows, number_of, top, lift):
    order = jax.random.permutation(jax.random.fold_in(stream_key, 1), number_of)
    boost = order
    for power in range(3):
        boost = boost * boost // number_of
    boost = boost * lift // number_of
    tickets = jax.random.randint(jax.random.fold_in(stream_key, 2), (rows, number_of), 0, 4096) + boost
    fixed_rows = jax.random.permutation(jax.random.fold_in(stream_key, 3), rows)[jnp.arange(number_of) % rows]
    tickets = jnp.where(jnp.arange(rows)[:, None] == fixed_rows[None, :], 1 << 14, tickets)
    priority = tickets * number_of + jnp.arange(number_of)
    return lax.top_k(priority.astype(jnp.int32), top)[1].astype(jnp.int32)


def normal_values(key, dims, scale, most, split=(), kind=jnp.bfloat16):
    result = jax.random.normal(key, dims, jnp.float32) * scale
    if len(split) > 0:
        result = block_scale(key, dims, split, -0.22, 0.18) * result
    return jnp.clip(result, min=-most, max=most).astype(kind)


def setup_inputs(seed: int = 0) -> dict:
    keys = jax.random.split(jax.random.key(seed), 6)
    grad_out = normal_values(keys[0], (TOKENS, D), 1.0, 6.0, ((0, 192),))
    expert_ids = picks_of(keys[1], TOKENS, EXPERTS, TOP, 1024)
    gate_values = jnp.clip(jnp.exp(math.log(0.5) - 3.224016 * jax.random.uniform(keys[2], (TOKENS, TOP), jnp.float32) ** block_scale(keys[2], (TOKENS, TOP), ((0, 192),), -0.2, 0.2)), 0.019897461, 0.5).astype(jnp.bfloat16)
    saved_hidden = normal_values(keys[3], (N_DP, N_EXPERT, SLOTS, FF), 0.1, 0.59765625, ((0, 4), (1, 48), (3, 4)))
    down_weight = normal_values(keys[4], (N_EXPERT, FF, D), FF ** -0.5, 0.15625, ((0, 48), (1, 4)))
    return dict(grad_out=grad_out, expert_ids=expert_ids, gate_values=gate_values, saved_hidden=saved_hidden, down_weight=down_weight)


def slot_table(route_ids, gate_rows, count):
    experts = jnp.arange(count, dtype=jnp.int32)
    hits = (route_ids[:, :, None] == experts[None, None, :]).astype(jnp.int32)
    member = lax.optimization_barrier(jnp.sum(hits, axis=1))
    gate_expert = lax.optimization_barrier(jnp.sum(jnp.where(hits > 0, gate_rows.astype(jnp.float32)[:, :, None], 0.0), axis=1))
    before = jnp.cumsum(member, axis=0) - member
    kept = member * (before < CAP).astype(jnp.int32)
    places = jnp.arange(CAP, dtype=jnp.int32)
    match = kept.T[:, None, :] * (before.T[:, None, :] == places[None, :, None]).astype(jnp.int32)
    positions = jnp.arange(route_ids.shape[0], dtype=jnp.int32)
    source_row = lax.optimization_barrier(jnp.sum(match * positions[None, None, :], axis=2)).astype(jnp.int32)
    filled = lax.optimization_barrier(jnp.sum(match, axis=2))
    slot_gate = lax.optimization_barrier(jnp.sum(match.astype(jnp.float32) * gate_expert.T[:, None, :], axis=2)).astype(jnp.bfloat16)
    return (source_row, filled, slot_gate, hits, kept, before)

def returned_grad(back, hits, kept, before):
    count = back.shape[0]
    spots = jnp.minimum(before, CAP - 1)
    picked = back[jnp.arange(count, dtype=jnp.int32)[None, :], spots]
    picked = jnp.where(kept > 0, picked, jnp.zeros((), picked.dtype))
    return lax.optimization_barrier(jnp.sum(hits.astype(picked.dtype) * picked[:, None, :], axis=2))

def pick_rows(grad_rows, source_row, filled):
    return jnp.where(filled[:, :, None] > 0, grad_rows[source_row], jnp.zeros((), grad_rows.dtype))

def reference(grad_out, expert_ids, gate_values, saved_hidden, down_weight):
    grads = grad_out.reshape(N_DP, N_EXPERT, TOK, D)
    routes = expert_ids.reshape(N_DP, N_EXPERT, TOK, TOP)
    gates = gate_values.reshape(N_DP, N_EXPERT, TOK, TOP)
    weight_wide = down_weight.astype(jnp.float32)
    table = partial(slot_table, count=N_EXPERT)

    def group(total, inputs):
        grad_group, route_group, gate_group, hidden_group = inputs
        source_row, filled, slot_gate, hits, kept, before = jax.vmap(table)(route_group, gate_group)
        outgoing = jax.vmap(pick_rows)(grad_group, source_row, filled)
        received = jnp.swapaxes(outgoing, 0, 1).reshape(N_EXPERT, N_EXPERT * CAP, D)
        gate_in = jnp.swapaxes(slot_gate, 0, 1).reshape(N_EXPERT, N_EXPERT * CAP).astype(jnp.float32)
        upstream = jnp.einsum('esd,efd->esf', received.astype(jnp.float32), weight_wide)
        hidden_grad = (gate_in[:, :, None] * upstream).astype(jnp.bfloat16)
        gate_part = lax.optimization_barrier(jnp.sum(hidden_group.astype(jnp.float32) * upstream, axis=2))
        weighted = (gate_in[:, :, None] * received.astype(jnp.float32)).astype(jnp.bfloat16)
        partial_grad = jnp.einsum('esf,esd->efd', hidden_group.astype(jnp.float32), weighted.astype(jnp.float32)).astype(jnp.bfloat16)
        back = jnp.swapaxes(gate_part.reshape(N_EXPERT, N_EXPERT, CAP), 0, 1)
        gate_grad = jax.vmap(returned_grad)(back, hits, kept, before)
        return (total + partial_grad.astype(jnp.float32), (gate_grad, hidden_grad))
    begin = jnp.zeros((N_EXPERT, FF, D), jnp.float32)
    total, (gate_grad, hidden_grad) = lax.scan(group, begin, (grads, routes, gates, saved_hidden))
    return (gate_grad.reshape(N_DP * N_EXPERT * TOK, TOP), hidden_grad, total)
```

```python
import jax
import jax.numpy as jnp
from jax import lax
from jax.sharding import PartitionSpec as P

CAP = 4


def on_device(grad_out, expert_ids, gate_values, saved_hidden, down_weight):
    count = lax.axis_size("expert")
    tokens, top = expert_ids.shape
    width = grad_out.shape[1]
    slot_count = count * CAP
    ids = expert_ids.T
    gates = gate_values.T.astype(jnp.float32)
    experts = jnp.arange(count, dtype=jnp.int32)
    hits = ids[:, None, :] == experts[None, :, None]
    member = jnp.sum(hits.astype(jnp.float32), axis=0)
    gate_expert = jnp.sum(jnp.where(hits, gates[:, None, :], 0.0), axis=0)
    order = jnp.arange(tokens, dtype=jnp.int32)
    earlier = (order[:, None] < order[None, :]).astype(jnp.bfloat16)
    before = lax.dot_general(
        member.astype(jnp.bfloat16), earlier, (((1,), (0,)), ((), ())),
        preferred_element_type=jnp.float32,
    )
    places = jnp.arange(CAP, dtype=jnp.float32)
    match = (member[:, None, :] > 0) & (before[:, None, :] == places[None, :, None])
    slot_gate = jnp.sum(jnp.where(match, gate_expert[:, None, :], 0.0), axis=2)
    pick = match.astype(jnp.bfloat16).reshape(slot_count, tokens)
    outgoing = lax.dot_general(
        pick, grad_out, (((1,), (0,)), ((), ())), preferred_element_type=jnp.float32
    ).astype(jnp.bfloat16)
    tail = jnp.broadcast_to(
        slot_gate.astype(jnp.bfloat16).reshape(slot_count, 1), (slot_count, 128)
    )
    payload = jnp.concatenate([outgoing, tail], axis=1).reshape(count, CAP, width + 128)
    landed = lax.all_to_all(payload, "expert", split_axis=0, concat_axis=0, tiled=True)
    landed = landed.reshape(slot_count, width + 128)
    arrived = landed[:, :width]
    gate_column = landed[:, width:width + 1].astype(jnp.float32)
    weight = down_weight[0]
    hidden = saved_hidden[0, 0]
    scaled = (gate_column * hidden.astype(jnp.float32)).astype(jnp.bfloat16)
    summed = lax.psum_scatter(
        lax.dot_general(
            arrived, scaled, (((0,), (0,)), ((), ())), preferred_element_type=jnp.float32
        ).astype(jnp.bfloat16),
        "dp", scatter_dimension=0, tiled=True,
    )
    upstream = lax.dot_general(
        arrived, weight, (((1,), (1,)), ((), ())), preferred_element_type=jnp.float32
    )
    hidden_grad = (gate_column * upstream).astype(jnp.bfloat16)
    gate_part = jnp.sum(hidden.astype(jnp.float32) * upstream, axis=1)
    gate_total = lax.psum(gate_part, "tensor")
    back = lax.all_to_all(
        gate_total.reshape(count, CAP), "expert", split_axis=0, concat_axis=0, tiled=True
    )
    picked = jnp.sum(jnp.where(match, back[:, :, None], 0.0), axis=1)
    gate_grad = jnp.sum(jnp.where(hits, picked[None], 0.0), axis=1).T
    down_grad = summed.astype(jnp.float32).T[None]
    return (gate_grad, hidden_grad[None, None], down_grad)


def solution(mesh):
    return jax.shard_map(
        on_device,
        mesh=mesh,
        in_specs=(
            P(("dp", "expert"), None),
            P(("dp", "expert"), None),
            P(("dp", "expert"), None),
            P("dp", "expert", None, "tensor"),
            P("expert", "tensor", None),
        ),
        out_specs=(
            P(("dp", "expert"), None),
            P("dp", "expert", None, "tensor"),
            P("expert", "tensor", "dp"),
        ),
        check_vma=False,
    )
```

```python
import jax
import jax.numpy as jnp
from jax import lax
from jax.experimental import pallas as pl
from jax.experimental.pallas import tpu as pltpu
from jax.sharding import PartitionSpec as P

CAP = 4
NZ = 12
NLO = 4
NX = 4
NT = 4
NE = NZ * NLO
GROUPS = 3
PER = NE // GROUPS
ROWS = PER * CAP
TOK = 128
LANE = 128
F32 = jnp.float32
BF16 = jnp.bfloat16
I32 = jnp.int32
MESH = pl.DeviceIdType.MESH


def offset_of(p):
    odd = p % 2
    return 6 + (1 - odd) * (p // 2) - odd * ((p + 1) // 2)


def iota(shape, dim):
    return lax.broadcasted_iota(I32, shape, dim)


def dot(a, b, dims=((1,), (0,))):
    return lax.dot_general(a, b, (dims, ((), ())), preferred_element_type=F32)


def kernel(ids_ref, gates_ref, grad_ref, hidden_ref, weight_ref,
           gg_ref, hg_ref, dw_ref,
           w_buf, pick_buf, g_buf, out_buf, in_buf, in2_buf,
           gout_buf, gin_buf, gate_buf, x_buf, xw_buf, xw2_buf, bw_buf, bw2_buf, h_buf,
           tout_buf, tin_buf, tsel_buf, part_buf, parts_buf,
           w_sem, own_sem, send_sem, a_sem, g_sem, h_sem, p1_sem, b_sem, p2_sem, t_sem, d_sem):
    x = lax.axis_index("dp")
    e = lax.axis_index("expert")
    t = lax.axis_index("tensor")
    z, lo = e // NLO, e % NLO
    hi, core = t // 2, t % 2

    def at_offset(dz, lo2):
        far = ((lo2 - lo) * (lo2 - lo)) // 9
        return {"dp": x, "expert": ((z + dz) % NZ) * NLO + lo2, "tensor": ((hi + far) % 2) * 2 + core}

    def x_peer(r):
        return {"dp": (x + r) % NX, "expert": e, "tensor": t}

    def t_peer(r):
        return {"dp": x, "expert": e, "tensor": (t + r) % NT}

    partner = {"dp": x, "expert": e, "tensor": hi * 2 + (1 - core)}

    barrier = pltpu.get_barrier_semaphore()

    def greet(p, carry):
        for lo2 in range(NLO):
            pl.semaphore_signal(barrier, inc=1, device_id=at_offset(offset_of(p), lo2), device_id_type=MESH)
        return carry

    lax.fori_loop(0, NZ - 1, greet, 0)
    for r in range(1, 4):
        pl.semaphore_signal(barrier, inc=1, device_id=at_offset(0, (lo + r) % NLO), device_id_type=MESH)
        pl.semaphore_signal(barrier, inc=1, device_id=x_peer(r), device_id_type=MESH)
        pl.semaphore_signal(barrier, inc=1, device_id=t_peer(r), device_id_type=MESH)

    w_copy = pltpu.make_async_copy(weight_ref, w_buf, w_sem)
    w_copy.start()

    row = iota((NE, TOK), 0)
    where_z = z + offset_of(row // NLO)
    expert = (where_z % NZ) * NLO + row % NLO
    member = jnp.zeros((NE, TOK), F32)
    gate = jnp.zeros((NE, TOK), F32)
    for k in range(8):
        hit = ids_ref[k:k + 1, :] == expert
        member = member + hit.astype(F32)
        gate = gate + jnp.where(hit, gates_ref[k:k + 1, :], 0.0)
    earlier = (iota((TOK, TOK), 0) < iota((TOK, TOK), 1)).astype(F32).astype(BF16)
    before = dot(member.astype(BF16), earlier)
    code = jnp.where((member > 0) & (before < CAP), before, -1.0)
    for c in range(CAP):
        picked = jnp.sum(jnp.where(code == c, gate, 0.0), axis=1, keepdims=True)
        wide = jnp.broadcast_to(picked, (NE, LANE))
        for s in range(NE):
            gout_buf[s, :, c * LANE:(c + 1) * LANE] = wide[s:s + 1, :]

    spread = (iota((NE * 16, NE), 0) // 16 == iota((NE * 16, NE), 1)).astype(F32).astype(BF16)
    code_wide = dot(spread, code.astype(BF16))
    place = iota((NE * 16, TOK), 0)
    chosen = code_wide == (place % CAP).astype(F32)
    part = (place // CAP) % 4
    for d in range(4):
        pick_buf[:, d * TOK:(d + 1) * TOK] = jnp.where(chosen & (part == d), 1.0, 0.0).astype(BF16)
    for q in range(4):
        for d in range(4):
            at = pl.multiple_of(q * 1024 + core * 512 + d * LANE, LANE)
            g_buf[d * TOK:(d + 1) * TOK, q * LANE:(q + 1) * LANE] = grad_ref[:, pl.ds(at, LANE)]
    for m in range(GROUPS):
        made = dot(pick_buf[m * 256:(m + 1) * 256, :], g_buf[...]).astype(BF16)
        for q in range(4):
            out_buf[q, m * 256:(m + 1) * 256, :] = made[:, q * LANE:(q + 1) * LANE]

    pl.semaphore_wait(barrier, 44 + 9)

    def block(ref, s):
        return ref.at[:, pl.ds(pl.multiple_of(s * 16, 16), 16), :]

    def send_rows(p, lo2, m):
        device = at_offset(offset_of(p), lo2)
        pltpu.make_async_remote_copy(
            src_ref=gout_buf.at[p * NLO + lo2], dst_ref=gin_buf.at[p * NLO + lo],
            send_sem=send_sem.at[1], recv_sem=g_sem.at[m], device_id=device, device_id_type=MESH).start()
        pltpu.make_async_remote_copy(
            src_ref=block(out_buf, p * NLO + lo2), dst_ref=block(in_buf, p * NLO + lo),
            send_sem=send_sem.at[0], recv_sem=a_sem.at[m], device_id=device, device_id_type=MESH).start()

    for m in range(GROUPS):
        def send_group(p, carry):
            for lo2 in range(NLO):
                send_rows(p, lo2, m)
            return carry

        lax.fori_loop(m * 4, m * 4 + (4 if m < 2 else 3), send_group, 0)
    for r in range(1, 4):
        send_rows(NZ - 1, (lo + r) % NLO, 2)
    mine = (NZ - 1) * NLO + lo
    pltpu.make_async_copy(block(out_buf, mine), block(in_buf, mine), a_sem.at[2]).start()
    pltpu.make_async_copy(gout_buf.at[mine], gin_buf.at[mine], g_sem.at[2]).start()
    for r in range(1, 4):
        pltpu.make_async_remote_copy(
            src_ref=hidden_ref, dst_ref=h_buf.at[r - 1],
            send_sem=send_sem.at[2], recv_sem=h_sem, device_id=x_peer(r), device_id_type=MESH).start()

    turn_row, turn_col = iota((256, 256), 0), iota((256, 256), 1)
    turn = ((turn_row // 64 == (turn_col // 4) % 4)
            & ((turn_row // 4) % 16 == turn_col // 16)
            & (turn_row % 4 == turn_col % 4)).astype(F32).astype(BF16)

    def natural(ref, m, xw, half):
        rows = jnp.concatenate([ref[q, m * 256:(m + 1) * 256, :] for q in range(4)], axis=1)
        turned = dot(turn, rows).astype(BF16)
        scale = gate_buf[...]
        for q in range(4):
            for d in range(4):
                piece = turned[d * ROWS:(d + 1) * ROWS, q * LANE:(q + 1) * LANE]
                at = pl.multiple_of(q * 1024 + half * 512 + d * LANE, LANE)
                x_buf[:, pl.ds(at, LANE)] = piece
                xw[m, q, :, d * LANE:(d + 1) * LANE] = (piece.astype(F32) * scale).astype(BF16)

    def wait_bytes(ref, sem):
        pltpu.make_async_copy(ref, ref, sem).wait()

    w_copy.wait()
    for m in range(GROUPS):
        rows = pl.ds(m * 256, 256)
        wait_bytes(in_buf.at[:, rows, :], a_sem.at[m])
        p1 = pltpu.make_async_remote_copy(
            src_ref=in_buf.at[:, rows, :], dst_ref=in2_buf.at[:, rows, :],
            send_sem=send_sem.at[3 + m], recv_sem=p1_sem.at[m], device_id=partner, device_id_type=MESH)
        p1.start()
        wait_bytes(gin_buf.at[pl.ds(m * PER, PER)], g_sem.at[m])
        for s in range(PER):
            for c in range(CAP):
                gate_buf[s * CAP + c:s * CAP + c + 1, :] = gin_buf[m * PER + s, :, c * LANE:(c + 1) * LANE]
        natural(in_buf, m, xw_buf, core)
        for r in range(1, 4):
            pltpu.make_async_remote_copy(
                src_ref=xw_buf.at[m, (x + r) % NX], dst_ref=bw_buf.at[m, r - 1],
                send_sem=send_sem.at[6 + m], recv_sem=b_sem.at[m], device_id=x_peer(r), device_id_type=MESH).start()
        p1.wait_recv()
        natural(in2_buf, m, xw2_buf, 1 - core)
        up = dot(x_buf[...], w_buf[...], ((1,), (1,)))
        wide_gate = jnp.concatenate([gate_buf[...]] * 3, axis=1)
        grads = (wide_gate * up).astype(BF16)
        for i in range(4):
            p = m * 4 + i
            at = pl.multiple_of(((z + NZ - offset_of(p)) % NZ) * 16, 16)
            hg_ref[pl.ds(at, 16), :] = grads[i * 16:(i + 1) * 16, :]
            rows16 = hidden_ref[pl.ds(at, 16), :]
            total = jnp.sum(rows16.astype(F32) * up[i * 16:(i + 1) * 16, :], axis=1, keepdims=True)
            wide = jnp.broadcast_to(total, (16, LANE))
            for s in range(4):
                for c in range(CAP):
                    tout_buf[p * NLO + s, :, c * LANE:(c + 1) * LANE] = wide[s * 4 + c:s * 4 + c + 1, :]

        def give_back(p, lo2):
            pltpu.make_async_remote_copy(
                src_ref=tout_buf.at[p * NLO + lo2], dst_ref=tin_buf.at[p * NLO + lo],
                send_sem=send_sem.at[9], recv_sem=t_sem,
                device_id=at_offset(NZ - offset_of(p), lo2), device_id_type=MESH).start()

        def back_group(p, carry):
            for lo2 in range(NLO):
                give_back(p, lo2)
            return carry

        lax.fori_loop(m * 4, m * 4 + (4 if m < 2 else 3), back_group, 0)
        if m == 2:
            for r in range(1, 4):
                give_back(NZ - 1, (lo + r) % NLO)
            pltpu.make_async_copy(tout_buf.at[mine], tin_buf.at[mine], t_sem).start()

        if m == 0:
            wait_bytes(h_buf, h_sem)
        wait_bytes(bw_buf.at[m], b_sem.at[m])
        p2 = pltpu.make_async_remote_copy(
            src_ref=bw_buf.at[m], dst_ref=bw2_buf.at[m],
            send_sem=send_sem.at[10 + m], recv_sem=p2_sem.at[m], device_id=partner, device_id_type=MESH)
        p2.start()
        pieces = []
        for i in range(4):
            at = pl.multiple_of(((z + NZ - offset_of(m * 4 + i)) % NZ) * 16, 16)
            pieces.append(at)
        held = jnp.concatenate(
            [hidden_ref[pl.ds(at, 16), :] for at in pieces]
            + [h_buf[r, pl.ds(at, 16), :] for r in range(3) for at in pieces], axis=0)
        first = jnp.concatenate([xw_buf[m, x]] + [bw_buf[m, r] for r in range(3)], axis=0)
        near = dot(held, first, ((0,), (0,)))
        lane0 = pl.ds(pl.multiple_of(core * 512, 512), 512)
        lane1 = pl.ds(pl.multiple_of((1 - core) * 512, 512), 512)
        dw_ref[:, lane0] = near if m == 0 else dw_ref[:, lane0] + near
        p2.wait_recv()
        second = jnp.concatenate([xw2_buf[m, x]] + [bw2_buf[m, r] for r in range(3)], axis=0)
        far_half = dot(held, second, ((0,), (0,)))
        dw_ref[:, lane1] = far_half if m == 0 else dw_ref[:, lane1] + far_half

    wait_bytes(tin_buf, t_sem)
    for s in range(NE):
        for c in range(CAP):
            tsel_buf[c, s:s + 1, :] = tin_buf[s, :, c * LANE:(c + 1) * LANE]
    value = jnp.zeros((NE, TOK), F32)
    for c in range(CAP):
        value = value + jnp.where(code == c, tsel_buf[c], 0.0)
    for k in range(8):
        hit = ids_ref[k:k + 1, :] == expert
        part_buf[k:k + 1, :] = jnp.sum(jnp.where(hit, value, 0.0), axis=0, keepdims=True)
    for r in range(1, 4):
        pltpu.make_async_remote_copy(
            src_ref=part_buf, dst_ref=parts_buf.at[r - 1],
            send_sem=send_sem.at[13], recv_sem=d_sem, device_id=t_peer(r), device_id_type=MESH).start()
    wait_bytes(parts_buf, d_sem)
    gg_ref[...] = (part_buf[...] + parts_buf[0]) + (parts_buf[1] + parts_buf[2])

    wait_bytes(out_buf.at[:, pl.ds(0, 47 * 16), :], send_sem.at[0])
    wait_bytes(gout_buf.at[pl.ds(0, 47)], send_sem.at[1])
    wait_bytes(h_buf, send_sem.at[2])
    for m in range(GROUPS):
        wait_bytes(in_buf.at[:, pl.ds(m * 256, 256), :], send_sem.at[3 + m])
        wait_bytes(bw_buf.at[m], send_sem.at[6 + m])
        wait_bytes(bw_buf.at[m], send_sem.at[10 + m])
    wait_bytes(tout_buf.at[pl.ds(0, 47)], send_sem.at[9])
    wait_bytes(parts_buf, send_sem.at[13])


def on_device(grad_out, expert_ids, gate_values, saved_hidden, down_weight):
    vmem = pl.BlockSpec(memory_space=pltpu.VMEM)
    dma = pltpu.SemaphoreType.DMA
    gg, hg, dw = pl.pallas_call(
        kernel,
        out_shape=(
            jax.ShapeDtypeStruct((8, TOK), F32),
            jax.ShapeDtypeStruct((192, 384), BF16),
            jax.ShapeDtypeStruct((384, 1024), F32),
        ),
        in_specs=[vmem, vmem, vmem, vmem, pl.BlockSpec(memory_space=pl.ANY)],
        out_specs=(vmem, vmem, vmem),
        scratch_shapes=[
            pltpu.VMEM((384, 4096), BF16),
            pltpu.VMEM((NE * 16, 512), BF16),
            pltpu.VMEM((512, 512), BF16),
            pltpu.VMEM((4, NE * 16, LANE), BF16),
            pltpu.VMEM((4, NE * 16, LANE), BF16),
            pltpu.VMEM((4, NE * 16, LANE), BF16),
            pltpu.VMEM((NE, 1, 512), F32),
            pltpu.VMEM((NE, 1, 512), F32),
            pltpu.VMEM((ROWS, LANE), F32),
            pltpu.VMEM((ROWS, 4096), BF16),
            pltpu.VMEM((GROUPS, 4, ROWS, 512), BF16),
            pltpu.VMEM((GROUPS, 4, ROWS, 512), BF16),
            pltpu.VMEM((GROUPS, 3, ROWS, 512), BF16),
            pltpu.VMEM((GROUPS, 3, ROWS, 512), BF16),
            pltpu.VMEM((3, 192, 384), BF16),
            pltpu.VMEM((NE, 1, 512), F32),
            pltpu.VMEM((NE, 1, 512), F32),
            pltpu.VMEM((CAP, NE, LANE), F32),
            pltpu.VMEM((8, TOK), F32),
            pltpu.VMEM((3, 8, TOK), F32),
            dma, dma, dma((14,)), dma((3,)), dma((3,)), dma, dma((3,)), dma((3,)), dma((3,)), dma, dma,
        ],
        compiler_params=pltpu.CompilerParams(
            collective_id=0, has_side_effects=True, vmem_limit_bytes=48 * 1024 * 1024
        ),
        name="exchange",
    )(expert_ids.T, gate_values.T.astype(F32), grad_out, saved_hidden[0, 0], down_weight[0])
    return (gg.T, hg[None, None], dw[None])


def solution(mesh):
    return jax.shard_map(
        on_device,
        mesh=mesh,
        in_specs=(
            P(("dp", "expert"), None),
            P(("dp", "expert"), None),
            P(("dp", "expert"), None),
            P("dp", "expert", None, "tensor"),
            P("expert", "tensor", None),
        ),
        out_specs=(
            P(("dp", "expert"), None),
            P("dp", "expert", None, "tensor"),
            P("expert", "tensor", "dp"),
        ),
        check_vma=False,
    )
```

```python
import jax
import jax.numpy as jnp
from jax import lax
from jax.experimental import pallas as pl
from jax.experimental.pallas import tpu as pltpu
from jax.sharding import PartitionSpec as P

CAP = 4
NZ = 12
NLO = 4
NX = 4
NT = 4
NE = NZ * NLO
GROUPS = 3
PER = NE // GROUPS
ROWS = PER * CAP
TOK = 128
LANE = 128
F32 = jnp.float32
BF16 = jnp.bfloat16
I32 = jnp.int32
MESH = pl.DeviceIdType.MESH


def offset_of(p):
    odd = p % 2
    return 6 + (1 - odd) * (p // 2) - odd * ((p + 1) // 2)


def iota(shape, dim):
    return lax.broadcasted_iota(I32, shape, dim)


def dot(a, b, dims=((1,), (0,))):
    return lax.dot_general(a, b, (dims, ((), ())), preferred_element_type=F32)


def crosses(a, b):
    square = (b - a) * (b - a)
    return square // 9 + ((square // 4) % 2) * ((a * (3 - a)) // 2)


def kernel(ids_in, gates_in, grad_in, hidden_in, weight_ref,
           gg_ref, hg_ref, dw_ref,
           ids_ref, gates_ref, grad_ref, hidden_ref, w_buf, pick_buf, g_buf, out_buf, in_buf, in2_buf,
           gout_buf, gin_buf, gate_buf, x_buf, xw_buf, xw2_buf, bw_buf, bw2_buf, h_buf,
           tout_buf, tin_buf, tsel_buf, part_buf, parts_buf,
           w_sem, load_sem, share_sem, send_sem, a_sem, g_sem, h_sem, p1_sem, b_sem, p2_sem, t_sem, d_sem):
    x = lax.axis_index("dp")
    e = lax.axis_index("expert")
    t = lax.axis_index("tensor")
    z, lo = e // NLO, e % NLO
    hi, core = t // 2, t % 2

    def at_offset(dz, lo2, far):
        return {"dp": x, "expert": ((z + dz) % NZ) * NLO + lo2, "tensor": ((hi + far) % 2) * 2 + core}

    def x_peer(r):
        return {"dp": (x + r) % NX, "expert": e, "tensor": t}

    def t_peer(r):
        return {"dp": x, "expert": e, "tensor": (t + r) % NT}

    partner = {"dp": x, "expert": e, "tensor": hi * 2 + (1 - core)}

    loads = [pltpu.make_async_copy(a, b, load_sem.at[i]) for i, (a, b) in enumerate(
        [(ids_in, ids_ref), (gates_in, gates_ref), (grad_in, grad_ref), (hidden_in, hidden_ref)])]
    for load in loads:
        load.start()
    w_copy = pltpu.make_async_copy(weight_ref, w_buf, w_sem)
    w_copy.start()

    barrier = pltpu.get_barrier_semaphore()
    across = (lo + 2) % NLO

    def greet_at(dz, lo2, far):
        pl.semaphore_signal(barrier, inc=1, device_id=at_offset(dz, lo2, far), device_id_type=MESH)

    def greet(p, carry):
        for lo2 in range(NLO):
            greet_at(offset_of(p), lo2, crosses(lo, lo2))
        greet_at(offset_of(p), across, crosses(across, lo))
        return carry

    lax.fori_loop(0, NZ - 1, greet, 0)
    greet_at(0, across, crosses(across, lo))
    for r in range(1, 4):
        greet_at(0, (lo + r) % NLO, crosses(lo, (lo + r) % NLO))
        pl.semaphore_signal(barrier, inc=1, device_id=x_peer(r), device_id_type=MESH)
        pl.semaphore_signal(barrier, inc=1, device_id=t_peer(r), device_id_type=MESH)

    row = iota((NE, TOK), 0)
    where_z = z + offset_of(row // NLO)
    expert = (where_z % NZ) * NLO + row % NLO
    member = jnp.zeros((NE, TOK), F32)
    gate = jnp.zeros((NE, TOK), F32)
    loads[0].wait()
    loads[1].wait()
    gate_rows = gates_ref[...].astype(F32)
    for k in range(8):
        hit = ids_ref[k:k + 1, :] == expert
        member = member + hit.astype(F32)
        gate = gate + jnp.where(hit, gate_rows[k:k + 1, :], 0.0)
    earlier = (iota((TOK, TOK), 0) < iota((TOK, TOK), 1)).astype(F32).astype(BF16)
    before = dot(member.astype(BF16), earlier)
    code = jnp.where((member > 0) & (before < CAP), before, -1.0)
    for c in range(CAP):
        picked = jnp.sum(jnp.where(code == c, gate, 0.0), axis=1, keepdims=True)
        wide = jnp.broadcast_to(picked, (NE, LANE))
        for s in range(NE):
            gout_buf[s, :, c * LANE:(c + 1) * LANE] = wide[s:s + 1, :]

    spread = (iota((NE * 16, NE), 0) // 16 == iota((NE * 16, NE), 1)).astype(F32).astype(BF16)
    code_wide = dot(spread, code.astype(BF16))
    place = iota((NE * 16, TOK), 0)
    chosen = code_wide == (place % CAP).astype(F32)
    part = (place // CAP) % 4
    for d in range(4):
        pick_buf[:, d * TOK:(d + 1) * TOK] = jnp.where(chosen & (part == d), 1.0, 0.0).astype(BF16)
    loads[2].wait()
    for q in range(4):
        for d in range(4):
            at = pl.multiple_of(q * 1024 + core * 512 + d * LANE, LANE)
            g_buf[d * TOK:(d + 1) * TOK, q * LANE:(q + 1) * LANE] = grad_ref[:, pl.ds(at, LANE)]
    for m in range(GROUPS):
        made = dot(pick_buf[m * 256:(m + 1) * 256, :], g_buf[...]).astype(BF16)
        for q in range(4):
            out_buf[q, m * 256:(m + 1) * 256, :] = made[:, q * LANE:(q + 1) * LANE]

    pl.semaphore_wait(barrier, 55 + 10)

    def block(ref, s, planes=slice(None)):
        return ref.at[planes, pl.ds(pl.multiple_of(s * 16, 16), 16), :]

    def send_rows(p, lo2, m):
        far = crosses(lo, lo2)
        device = at_offset(offset_of(p), lo2, far)
        planes = pl.ds(((hi + far) % 2) * 2, 2) if m == 0 else slice(None)
        pltpu.make_async_remote_copy(
            src_ref=gout_buf.at[p * NLO + lo2], dst_ref=gin_buf.at[p * NLO + lo],
            send_sem=send_sem.at[1], recv_sem=g_sem.at[m], device_id=device, device_id_type=MESH).start()
        pltpu.make_async_remote_copy(
            src_ref=block(out_buf, p * NLO + lo2, planes), dst_ref=block(in_buf, p * NLO + lo, planes),
            send_sem=send_sem.at[0 if m == 0 else 14], recv_sem=a_sem.at[m], device_id=device, device_id_type=MESH).start()

    for m in range(GROUPS):
        def send_group(p, carry):
            for lo2 in range(NLO):
                send_rows(p, lo2, m)
            return carry

        lax.fori_loop(m * 4, m * 4 + (4 if m < 2 else 3), send_group, 0)
    for r in range(1, 4):
        send_rows(NZ - 1, (lo + r) % NLO, 2)
    mine = (NZ - 1) * NLO + lo
    pltpu.make_async_copy(block(out_buf, mine), block(in_buf, mine), a_sem.at[2]).start()
    pltpu.make_async_copy(gout_buf.at[mine], gin_buf.at[mine], g_sem.at[2]).start()
    for r in range(1, 4):
        pltpu.make_async_remote_copy(
            src_ref=hidden_in, dst_ref=h_buf.at[r - 1],
            send_sem=send_sem.at[2], recv_sem=h_sem, device_id=x_peer(r), device_id_type=MESH).start()

    turn_row, turn_col = iota((256, 256), 0), iota((256, 256), 1)
    turn = ((turn_row // 64 == (turn_col // 4) % 4)
            & ((turn_row // 4) % 16 == turn_col // 16)
            & (turn_row % 4 == turn_col % 4)).astype(F32).astype(BF16)

    def natural(ref, m, xw, half):
        rows = jnp.concatenate([ref[q, m * 256:(m + 1) * 256, :] for q in range(4)], axis=1)
        turned = dot(turn, rows).astype(BF16)
        scale = gate_buf[...]
        for q in range(4):
            for d in range(4):
                piece = turned[d * ROWS:(d + 1) * ROWS, q * LANE:(q + 1) * LANE]
                at = pl.multiple_of(q * 1024 + half * 512 + d * LANE, LANE)
                x_buf[:, pl.ds(at, LANE)] = piece
                xw[m, q, :, d * LANE:(d + 1) * LANE] = (piece.astype(F32) * scale).astype(BF16)

    def wait_bytes(ref, sem):
        pltpu.make_async_copy(ref, ref, sem).wait()

    loads[3].wait()
    w_copy.wait()
    for m in range(GROUPS):
        rows = pl.ds(m * 256, 256)
        if m == 0:
            got, lacking = pl.ds(hi * 2, 2), pl.ds((1 - hi) * 2, 2)
            wait_bytes(in_buf.at[got, rows, :], a_sem.at[m])
            share = pltpu.make_async_remote_copy(
                src_ref=in_buf.at[got, rows, :], dst_ref=in_buf.at[got, rows, :],
                send_sem=send_sem.at[15], recv_sem=share_sem, device_id=t_peer(2), device_id_type=MESH)
            share.start()
            wait_bytes(in_buf.at[lacking, rows, :], share_sem)
        else:
            wait_bytes(in_buf.at[:, rows, :], a_sem.at[m])
        p1 = pltpu.make_async_remote_copy(
            src_ref=in_buf.at[:, rows, :], dst_ref=in2_buf.at[:, rows, :],
            send_sem=send_sem.at[3 + m], recv_sem=p1_sem.at[m], device_id=partner, device_id_type=MESH)
        p1.start()
        wait_bytes(gin_buf.at[pl.ds(m * PER, PER)], g_sem.at[m])
        for s in range(PER):
            for c in range(CAP):
                gate_buf[s * CAP + c:s * CAP + c + 1, :] = gin_buf[m * PER + s, :, c * LANE:(c + 1) * LANE]
        natural(in_buf, m, xw_buf, core)
        for r in range(1, 4):
            pltpu.make_async_remote_copy(
                src_ref=xw_buf.at[m, (x + r) % NX], dst_ref=bw_buf.at[m, r - 1],
                send_sem=send_sem.at[6 + m], recv_sem=b_sem.at[m], device_id=x_peer(r), device_id_type=MESH).start()
        p1.wait_recv()
        natural(in2_buf, m, xw2_buf, 1 - core)
        up = dot(x_buf[...], w_buf[...], ((1,), (1,)))
        wide_gate = jnp.concatenate([gate_buf[...]] * 3, axis=1)
        grads = (wide_gate * up).astype(BF16)
        for i in range(4):
            p = m * 4 + i
            at = pl.multiple_of(((z + NZ - offset_of(p)) % NZ) * 16, 16)
            hg_ref[pl.ds(at, 16), :] = grads[i * 16:(i + 1) * 16, :]
            rows16 = hidden_ref[pl.ds(at, 16), :]
            total = jnp.sum(rows16.astype(F32) * up[i * 16:(i + 1) * 16, :], axis=1, keepdims=True)
            wide = jnp.broadcast_to(total, (16, LANE))
            for s in range(4):
                for c in range(CAP):
                    tout_buf[p * NLO + s, :, c * LANE:(c + 1) * LANE] = wide[s * 4 + c:s * 4 + c + 1, :]

        def give_back(p, lo2):
            pltpu.make_async_remote_copy(
                src_ref=tout_buf.at[p * NLO + lo2], dst_ref=tin_buf.at[p * NLO + lo],
                send_sem=send_sem.at[9], recv_sem=t_sem,
                device_id=at_offset(NZ - offset_of(p), lo2, crosses(lo2, lo)), device_id_type=MESH).start()

        def back_group(p, carry):
            for lo2 in range(NLO):
                give_back(p, lo2)
            return carry

        lax.fori_loop(m * 4, m * 4 + (4 if m < 2 else 3), back_group, 0)
        if m == 2:
            for r in range(1, 4):
                give_back(NZ - 1, (lo + r) % NLO)
            pltpu.make_async_copy(tout_buf.at[mine], tin_buf.at[mine], t_sem).start()

        if m == 0:
            wait_bytes(h_buf, h_sem)
        wait_bytes(bw_buf.at[m], b_sem.at[m])
        p2 = pltpu.make_async_remote_copy(
            src_ref=bw_buf.at[m], dst_ref=bw2_buf.at[m],
            send_sem=send_sem.at[10 + m], recv_sem=p2_sem.at[m], device_id=partner, device_id_type=MESH)
        p2.start()
        pieces = []
        for i in range(4):
            at = pl.multiple_of(((z + NZ - offset_of(m * 4 + i)) % NZ) * 16, 16)
            pieces.append(at)
        held = jnp.concatenate(
            [hidden_ref[pl.ds(at, 16), :] for at in pieces]
            + [h_buf[r, pl.ds(at, 16), :] for r in range(3) for at in pieces], axis=0)
        first = jnp.concatenate([xw_buf[m, x]] + [bw_buf[m, r] for r in range(3)], axis=0)
        near = dot(held, first, ((0,), (0,)))
        lane0 = pl.ds(pl.multiple_of(core * 512, 512), 512)
        lane1 = pl.ds(pl.multiple_of((1 - core) * 512, 512), 512)
        dw_ref[:, lane0] = near if m == 0 else dw_ref[:, lane0] + near
        p2.wait_recv()
        second = jnp.concatenate([xw2_buf[m, x]] + [bw2_buf[m, r] for r in range(3)], axis=0)
        far_half = dot(held, second, ((0,), (0,)))
        dw_ref[:, lane1] = far_half if m == 0 else dw_ref[:, lane1] + far_half

    wait_bytes(tin_buf, t_sem)
    for s in range(NE):
        for c in range(CAP):
            tsel_buf[c, s:s + 1, :] = tin_buf[s, :, c * LANE:(c + 1) * LANE]
    value = jnp.zeros((NE, TOK), F32)
    for c in range(CAP):
        value = value + jnp.where(code == c, tsel_buf[c], 0.0)
    for k in range(8):
        hit = ids_ref[k:k + 1, :] == expert
        part_buf[k:k + 1, :] = jnp.sum(jnp.where(hit, value, 0.0), axis=0, keepdims=True)
    for r in range(1, 4):
        pltpu.make_async_remote_copy(
            src_ref=part_buf, dst_ref=parts_buf.at[r - 1],
            send_sem=send_sem.at[13], recv_sem=d_sem, device_id=t_peer(r), device_id_type=MESH).start()
    wait_bytes(parts_buf, d_sem)
    gg_ref[...] = (part_buf[...] + parts_buf[0]) + (parts_buf[1] + parts_buf[2])

    wait_bytes(out_buf.at[pl.ds(0, 2), pl.ds(0, 256), :], send_sem.at[0])
    wait_bytes(out_buf.at[:, pl.ds(0, 31 * 16), :], send_sem.at[14])
    wait_bytes(in_buf.at[pl.ds(0, 2), pl.ds(0, 256), :], send_sem.at[15])
    wait_bytes(gout_buf.at[pl.ds(0, 47)], send_sem.at[1])
    wait_bytes(h_buf, send_sem.at[2])
    for m in range(GROUPS):
        wait_bytes(in_buf.at[:, pl.ds(m * 256, 256), :], send_sem.at[3 + m])
        wait_bytes(bw_buf.at[m], send_sem.at[6 + m])
        wait_bytes(bw_buf.at[m], send_sem.at[10 + m])
    wait_bytes(tout_buf.at[pl.ds(0, 47)], send_sem.at[9])
    wait_bytes(parts_buf, send_sem.at[13])


def flush(gg_ref, hg_ref, dw_ref, gg_out, hg_out, dw_out, sem):
    moves = [pltpu.make_async_copy(a, b, sem.at[i]) for i, (a, b) in enumerate(
        [(dw_ref, dw_out), (hg_ref, hg_out), (gg_ref, gg_out)])]
    for move in moves:
        move.start()
    for move in moves:
        move.wait()


def on_device(grad_out, expert_ids, gate_values, saved_hidden, down_weight):
    vmem = pl.BlockSpec(memory_space=pltpu.VMEM)
    hbm = pl.BlockSpec(memory_space=pltpu.HBM)
    dma = pltpu.SemaphoreType.DMA
    gg, hg, dw = pl.pallas_call(
        kernel,
        out_shape=(
            pltpu.VMEM((8, TOK), F32),
            pltpu.VMEM((192, 384), BF16),
            pltpu.VMEM((384, 1024), F32),
        ),
        in_specs=[hbm] * 5,
        out_specs=(vmem, vmem, vmem),
        scratch_shapes=[
            pltpu.VMEM((8, TOK), I32),
            pltpu.VMEM((8, TOK), BF16),
            pltpu.VMEM((TOK, 4096), BF16),
            pltpu.VMEM((192, 384), BF16),
            pltpu.VMEM((384, 4096), BF16),
            pltpu.VMEM((NE * 16, 512), BF16),
            pltpu.VMEM((512, 512), BF16),
            pltpu.VMEM((4, NE * 16, LANE), BF16),
            pltpu.VMEM((4, NE * 16, LANE), BF16),
            pltpu.VMEM((4, NE * 16, LANE), BF16),
            pltpu.VMEM((NE, 1, 512), F32),
            pltpu.VMEM((NE, 1, 512), F32),
            pltpu.VMEM((ROWS, LANE), F32),
            pltpu.VMEM((ROWS, 4096), BF16),
            pltpu.VMEM((GROUPS, 4, ROWS, 512), BF16),
            pltpu.VMEM((GROUPS, 4, ROWS, 512), BF16),
            pltpu.VMEM((GROUPS, 3, ROWS, 512), BF16),
            pltpu.VMEM((GROUPS, 3, ROWS, 512), BF16),
            pltpu.VMEM((3, 192, 384), BF16),
            pltpu.VMEM((NE, 1, 512), F32),
            pltpu.VMEM((NE, 1, 512), F32),
            pltpu.VMEM((CAP, NE, LANE), F32),
            pltpu.VMEM((8, TOK), F32),
            pltpu.VMEM((3, 8, TOK), F32),
            dma, dma((4,)), dma, dma((16,)), dma((3,)), dma((3,)), dma, dma((3,)), dma((3,)), dma((3,)), dma, dma,
        ],
        compiler_params=pltpu.CompilerParams(
            collective_id=0, has_side_effects=True, vmem_limit_bytes=60 * 1024 * 1024
        ),
        name="exchange",
    )(expert_ids.T, gate_values.T, grad_out, saved_hidden[0, 0], down_weight[0])
    gg, hg, dw = pl.pallas_call(
        flush,
        out_shape=(
            jax.ShapeDtypeStruct((8, TOK), F32),
            jax.ShapeDtypeStruct((192, 384), BF16),
            jax.ShapeDtypeStruct((384, 1024), F32),
        ),
        in_specs=[vmem] * 3,
        out_specs=(hbm,) * 3,
        scratch_shapes=[dma((3,))],
        compiler_params=pltpu.CompilerParams(vmem_limit_bytes=1024 * 1024),
        name="flush",
    )(gg, hg, dw)
    return (gg.T, hg[None, None], dw[None])


def solution(mesh):
    return jax.shard_map(
        on_device,
        mesh=mesh,
        in_specs=(
            P(("dp", "expert"), None),
            P(("dp", "expert"), None),
            P(("dp", "expert"), None),
            P("dp", "expert", None, "tensor"),
            P("expert", "tensor", None),
        ),
        out_specs=(
            P(("dp", "expert"), None),
            P("dp", "expert", None, "tensor"),
            P("expert", "tensor", "dp"),
        ),
        check_vma=False,
    )
```

```python
import jax
import jax.numpy as jnp
from jax import lax
from jax.experimental import pallas as pl
from jax.experimental.pallas import tpu as pltpu
from jax.sharding import PartitionSpec as P

CAP = 4
NZ = 12
NLO = 4
NX = 4
NT = 4
NE = NZ * NLO
GROUPS = 3
PER = NE // GROUPS
ROWS = PER * CAP
TOK = 128
LANE = 128
F32 = jnp.float32
BF16 = jnp.bfloat16
I32 = jnp.int32
MESH = pl.DeviceIdType.MESH


def offset_of(position):
    p = (position + 8) % NZ
    odd = p % 2
    return 6 + (1 - odd) * (p // 2) - odd * ((p + 1) // 2)


def iota(shape, dim):
    return lax.broadcasted_iota(I32, shape, dim)


def dot(a, b, dims=((1,), (0,))):
    return lax.dot_general(a, b, (dims, ((), ())), preferred_element_type=F32)


def crosses(a, b):
    square = (b - a) * (b - a)
    return square // 9 + ((square // 4) % 2) * ((a * (3 - a)) // 2)


def kernel(ids_in, gates_in, grad_in, hidden_in, weight_ref,
           gg_ref, hg_ref, dw_ref,
           ids_ref, gates_ref, grad_ref, hidden_ref, w_buf, pick_buf, g_buf, out_buf, in_buf, in2_buf,
           gout_buf, gin_buf, gate_buf, x_buf, xw_buf, xw2_buf, bw_buf, bw2_buf, h_buf,
           tout_buf, tin_buf, tsel_buf, part_buf, parts_buf,
           w_sem, load_sem, share_sem, send_sem, a_sem, g_sem, h_sem, p1_sem, b_sem, p2_sem, t_sem, d_sem):
    x = lax.axis_index("dp")
    e = lax.axis_index("expert")
    t = lax.axis_index("tensor")
    z, lo = e // NLO, e % NLO
    hi, core = t // 2, t % 2

    def at_offset(dz, lo2, far):
        return {"dp": x, "expert": ((z + dz) % NZ) * NLO + lo2, "tensor": ((hi + far) % 2) * 2 + core}

    def x_peer(r):
        return {"dp": (x + r) % NX, "expert": e, "tensor": t}

    def t_peer(r):
        return {"dp": x, "expert": e, "tensor": (t + r) % NT}

    partner = {"dp": x, "expert": e, "tensor": hi * 2 + (1 - core)}

    loads = [pltpu.make_async_copy(a, b, load_sem.at[i]) for i, (a, b) in enumerate(
        [(ids_in, ids_ref), (gates_in, gates_ref), (grad_in, grad_ref), (hidden_in, hidden_ref)])]
    for load in loads:
        load.start()
    w_copy = pltpu.make_async_copy(weight_ref, w_buf, w_sem)
    w_copy.start()

    barrier = pltpu.get_barrier_semaphore()

    def greet_at(dz, lo2, hi2):
        pl.semaphore_signal(barrier, inc=1, device_id_type=MESH, device_id={
            "dp": x, "expert": ((z + dz) % NZ) * NLO + lo2, "tensor": hi2 * 2 + core})

    def greet(dz, carry):
        for lo2 in range(NLO):
            for hi2 in range(2):
                greet_at(dz, lo2, hi2)
        return carry

    lax.fori_loop(1, NZ, greet, 0)
    for r in range(1, 4):
        for hi2 in range(2):
            greet_at(0, (lo + r) % NLO, hi2)
    greet_at(0, lo, 1 - hi)
    pl.semaphore_signal(barrier, inc=1, device_id=partner, device_id_type=MESH)
    for r in range(1, 4):
        pl.semaphore_signal(barrier, inc=1, device_id=x_peer(r), device_id_type=MESH)

    row = iota((NE, TOK), 0)
    where_z = z + offset_of(row // NLO)
    expert = (where_z % NZ) * NLO + row % NLO
    member = jnp.zeros((NE, TOK), F32)
    gate = jnp.zeros((NE, TOK), F32)
    loads[0].wait()
    loads[1].wait()
    gate_rows = gates_ref[...].astype(F32)
    for k in range(8):
        hit = ids_ref[k:k + 1, :] == expert
        member = member + hit.astype(F32)
        gate = gate + jnp.where(hit, gate_rows[k:k + 1, :], 0.0)
    earlier = (iota((TOK, TOK), 0) < iota((TOK, TOK), 1)).astype(F32).astype(BF16)
    before = dot(member.astype(BF16), earlier)
    code = jnp.where((member > 0) & (before < CAP), before, -1.0)
    for c in range(CAP):
        picked = jnp.sum(jnp.where(code == c, gate, 0.0), axis=1, keepdims=True)
        wide = jnp.broadcast_to(picked, (NE, LANE))
        for s in range(NE):
            gout_buf[s, :, c * LANE:(c + 1) * LANE] = wide[s:s + 1, :]

    spread = (iota((NE * 16, NE), 0) // 16 == iota((NE * 16, NE), 1)).astype(F32).astype(BF16)
    code_wide = dot(spread, code.astype(BF16))
    place = iota((NE * 16, TOK), 0)
    chosen = code_wide == (place % CAP).astype(F32)
    part = (place // CAP) % 4
    for d in range(4):
        pick_buf[:, d * TOK:(d + 1) * TOK] = jnp.where(chosen & (part == d), 1.0, 0.0).astype(BF16)
    loads[2].wait()
    for q in range(4):
        for d in range(4):
            at = pl.multiple_of(q * 1024 + core * 512 + d * LANE, LANE)
            g_buf[d * TOK:(d + 1) * TOK, q * LANE:(q + 1) * LANE] = grad_ref[:, pl.ds(at, LANE)]
    for m in range(GROUPS):
        made = dot(pick_buf[m * 256:(m + 1) * 256, :], g_buf[...]).astype(BF16)
        for q in range(4):
            out_buf[q, m * 256:(m + 1) * 256, :] = made[:, q * LANE:(q + 1) * LANE]

    pl.semaphore_wait(barrier, 95 + 4)

    def block(ref, s, planes=slice(None)):
        return ref.at[planes, pl.ds(pl.multiple_of(s * 16, 16), 16), :]

    def send_rows(p, lo2, m):
        far = crosses(lo, lo2)
        device = at_offset(offset_of(p), lo2, far)
        planes = pl.ds(((hi + far) % 2) * 2, 2) if m == 1 else slice(None)
        rows_sem = a_sem.at[p] if m == 2 else a_sem.at[m]
        pltpu.make_async_remote_copy(
            src_ref=gout_buf.at[p * NLO + lo2], dst_ref=gin_buf.at[p * NLO + lo],
            send_sem=send_sem.at[1], recv_sem=g_sem.at[m], device_id=device, device_id_type=MESH).start()
        pltpu.make_async_remote_copy(
            src_ref=block(out_buf, p * NLO + lo2, planes), dst_ref=block(in_buf, p * NLO + lo, planes),
            send_sem=send_sem.at[0 if m == 1 else 14], recv_sem=rows_sem, device_id=device,
            device_id_type=MESH).start()

    def send_group(m):
        def body(p, carry):
            for lo2 in range(NLO):
                send_rows(p, lo2, m)
            return carry
        return body

    mine = 3 * NLO + lo
    lax.fori_loop(4, 8, send_group(1), 0)
    for r in range(1, 4):
        send_rows(3, (lo + r) % NLO, 0)
    lax.fori_loop(0, 3, send_group(0), 0)
    pltpu.make_async_copy(block(out_buf, mine), block(in_buf, mine), a_sem.at[0]).start()
    pltpu.make_async_copy(gout_buf.at[mine], gin_buf.at[mine], g_sem.at[0]).start()
    for r in range(1, 4):
        pltpu.make_async_remote_copy(
            src_ref=hidden_in, dst_ref=h_buf.at[r - 1],
            send_sem=send_sem.at[2], recv_sem=h_sem, device_id=x_peer(r), device_id_type=MESH).start()
    for p in range(8, 12):
        for lo2 in range(NLO):
            send_rows(p, lo2, 2)

    turn_row, turn_col = iota((256, 256), 0), iota((256, 256), 1)
    turn = ((turn_row // 64 == (turn_col // 4) % 4)
            & ((turn_row // 4) % 16 == turn_col // 16)
            & (turn_row % 4 == turn_col % 4)).astype(F32).astype(BF16)

    def natural(ref, m, xw, half):
        rows = jnp.concatenate([ref[q, m * 256:(m + 1) * 256, :] for q in range(4)], axis=1)
        turned = dot(turn, rows).astype(BF16)
        scale = gate_buf[...]
        for q in range(4):
            for d in range(4):
                piece = turned[d * ROWS:(d + 1) * ROWS, q * LANE:(q + 1) * LANE]
                at = pl.multiple_of(q * 1024 + half * 512 + d * LANE, LANE)
                x_buf[:, pl.ds(at, LANE)] = piece
                xw[m, q, :, d * LANE:(d + 1) * LANE] = (piece.astype(F32) * scale).astype(BF16)

    def wait_bytes(ref, sem):
        pltpu.make_async_copy(ref, ref, sem).wait()

    def core_copy(m, rows):
        return pltpu.make_async_remote_copy(
            src_ref=in_buf.at[:, rows, :], dst_ref=in2_buf.at[:, rows, :],
            send_sem=send_sem.at[3 + m], recv_sem=p1_sem.at[m], device_id=partner, device_id_type=MESH)

    def rows_of(m):
        return [pl.multiple_of(((z + NZ - offset_of(m * 4 + i)) % NZ) * 16, 16) for i in range(4)]

    def take_rows(m):
        rows = pl.ds(m * 256, 256)
        if m == 2:
            for p in range(8, 12):
                part_rows = pl.ds(p * 64, 64)
                wait_bytes(in_buf.at[:, part_rows, :], a_sem.at[p])
                core_copy(m, part_rows).start()
        elif m == 1:
            got, lacking = pl.ds(hi * 2, 2), pl.ds((1 - hi) * 2, 2)
            wait_bytes(in_buf.at[got, rows, :], a_sem.at[m])
            pltpu.make_async_remote_copy(
                src_ref=in_buf.at[got, rows, :], dst_ref=in_buf.at[got, rows, :],
                send_sem=send_sem.at[15], recv_sem=share_sem, device_id=t_peer(2), device_id_type=MESH).start()
            wait_bytes(in_buf.at[lacking, rows, :], share_sem)
            core_copy(m, rows).start()
        else:
            wait_bytes(in_buf.at[:, rows, :], a_sem.at[m])
            core_copy(m, rows).start()
        wait_bytes(gin_buf.at[pl.ds(m * PER, PER)], g_sem.at[m])
        for s in range(PER):
            for c in range(CAP):
                gate_buf[s * CAP + c:s * CAP + c + 1, :] = gin_buf[m * PER + s, :, c * LANE:(c + 1) * LANE]
        natural(in_buf, m, xw_buf, core)
        for r in range(1, 4):
            pltpu.make_async_remote_copy(
                src_ref=xw_buf.at[m, (x + r) % NX], dst_ref=bw_buf.at[m, r - 1],
                send_sem=send_sem.at[6 + m], recv_sem=b_sem.at[m], device_id=x_peer(r), device_id_type=MESH).start()

    def give_back(p, lo2):
        for hi2 in range(2):
            pltpu.make_async_remote_copy(
                src_ref=tout_buf.at[p * NLO + lo2], dst_ref=tin_buf.at[hi, p * NLO + lo],
                send_sem=send_sem.at[9 if hi2 == 0 else 16], recv_sem=t_sem, device_id_type=MESH, device_id={
                    "dp": x, "expert": ((z + NZ - offset_of(p)) % NZ) * NLO + lo2,
                    "tensor": hi2 * 2 + core}).start()

    def back_group(p, carry):
        for lo2 in range(NLO):
            give_back(p, lo2)
        return carry

    def up_and_back(m):
        wait_bytes(in2_buf.at[:, pl.ds(m * 256, 256), :], p1_sem.at[m])
        natural(in2_buf, m, xw2_buf, 1 - core)
        up = dot(x_buf[...], w_buf[...], ((1,), (1,)))
        wide_gate = jnp.concatenate([gate_buf[...]] * 3, axis=1)
        grads = (wide_gate * up).astype(BF16)
        for i, at in enumerate(rows_of(m)):
            p = m * 4 + i
            rows16 = hidden_ref[pl.ds(at, 16), :]
            total = jnp.sum(rows16.astype(F32) * up[i * 16:(i + 1) * 16, :], axis=1, keepdims=True)
            wide = jnp.broadcast_to(total, (16, LANE))
            for s in range(4):
                for c in range(CAP):
                    tout_buf[p * NLO + s, :, c * LANE:(c + 1) * LANE] = wide[s * 4 + c:s * 4 + c + 1, :]
            hg_ref[pl.ds(at, 16), :] = grads[i * 16:(i + 1) * 16, :]
        if m == 0:
            for r in range(1, 4):
                give_back(3, (lo + r) % NLO)
            pltpu.make_async_copy(tout_buf.at[mine], tin_buf.at[hi, mine], t_sem).start()
            pltpu.make_async_remote_copy(
                src_ref=tout_buf.at[mine], dst_ref=tin_buf.at[hi, mine],
                send_sem=send_sem.at[17], recv_sem=t_sem, device_id=t_peer(2), device_id_type=MESH).start()
        lax.fori_loop(m * 4, m * 4 + (3 if m == 0 else 4), back_group, 0)

    def pass_on(m):
        wait_bytes(bw_buf.at[m], b_sem.at[m])
        pltpu.make_async_remote_copy(
            src_ref=bw_buf.at[m], dst_ref=bw2_buf.at[m],
            send_sem=send_sem.at[10 + m], recv_sem=p2_sem.at[m], device_id=partner, device_id_type=MESH).start()

    def contract(m):
        at_rows = rows_of(m)
        held = jnp.concatenate(
            [hidden_ref[pl.ds(at, 16), :] for at in at_rows]
            + [h_buf[r, pl.ds(at, 16), :] for r in range(3) for at in at_rows], axis=0)
        first = jnp.concatenate([xw_buf[m, x]] + [bw_buf[m, r] for r in range(3)], axis=0)
        near = dot(held, first, ((0,), (0,)))
        lane0 = pl.ds(pl.multiple_of(core * 512, 512), 512)
        lane1 = pl.ds(pl.multiple_of((1 - core) * 512, 512), 512)
        dw_ref[:, lane0] = near if m == 0 else dw_ref[:, lane0] + near
        wait_bytes(bw2_buf.at[m], p2_sem.at[m])
        second = jnp.concatenate([xw2_buf[m, x]] + [bw2_buf[m, r] for r in range(3)], axis=0)
        far_half = dot(held, second, ((0,), (0,)))
        dw_ref[:, lane1] = far_half if m == 0 else dw_ref[:, lane1] + far_half

    loads[3].wait()
    w_copy.wait()
    take_rows(0)
    up_and_back(0)
    pass_on(0)
    take_rows(1)
    up_and_back(1)
    wait_bytes(h_buf, h_sem)
    contract(0)
    pass_on(1)
    take_rows(2)
    up_and_back(2)
    contract(1)
    pass_on(2)
    contract(2)

    wait_bytes(tin_buf, t_sem)
    for s in range(NE):
        for c in range(CAP):
            lanes = slice(c * LANE, (c + 1) * LANE)
            tsel_buf[c, s:s + 1, :] = tin_buf[0, s, :, lanes] + tin_buf[1, s, :, lanes]
    value = jnp.zeros((NE, TOK), F32)
    for c in range(CAP):
        value = value + jnp.where(code == c, tsel_buf[c], 0.0)
    for k in range(8):
        hit = ids_ref[k:k + 1, :] == expert
        part_buf[k:k + 1, :] = jnp.sum(jnp.where(hit, value, 0.0), axis=0, keepdims=True)
    last = pltpu.make_async_remote_copy(
        src_ref=part_buf, dst_ref=parts_buf,
        send_sem=send_sem.at[13], recv_sem=d_sem, device_id=partner, device_id_type=MESH)
    last.start()
    last.wait()
    gg_ref[...] = part_buf[...] + parts_buf[...]

    wait_bytes(out_buf.at[pl.ds(0, 2), pl.ds(0, 256), :], send_sem.at[0])
    wait_bytes(out_buf.at[:, pl.ds(0, 31 * 16), :], send_sem.at[14])
    wait_bytes(in_buf.at[pl.ds(0, 2), pl.ds(0, 256), :], send_sem.at[15])
    wait_bytes(gout_buf.at[pl.ds(0, 47)], send_sem.at[1])
    wait_bytes(h_buf, send_sem.at[2])
    for m in range(GROUPS):
        wait_bytes(in_buf.at[:, pl.ds(m * 256, 256), :], send_sem.at[3 + m])
        wait_bytes(bw_buf.at[m], send_sem.at[6 + m])
        wait_bytes(bw_buf.at[m], send_sem.at[10 + m])
    wait_bytes(tout_buf.at[pl.ds(0, 47)], send_sem.at[9])
    wait_bytes(tout_buf.at[pl.ds(0, 47)], send_sem.at[16])
    wait_bytes(tout_buf.at[0], send_sem.at[17])


def flush(gg_ref, hg_ref, dw_ref, gg_out, hg_out, dw_out, sem):
    moves = [pltpu.make_async_copy(a, b, sem.at[i]) for i, (a, b) in enumerate(
        [(dw_ref, dw_out), (hg_ref, hg_out), (gg_ref, gg_out)])]
    for move in moves:
        move.start()
    for move in moves:
        move.wait()


def on_device(grad_out, expert_ids, gate_values, saved_hidden, down_weight):
    vmem = pl.BlockSpec(memory_space=pltpu.VMEM)
    hbm = pl.BlockSpec(memory_space=pltpu.HBM)
    dma = pltpu.SemaphoreType.DMA
    gg, hg, dw = pl.pallas_call(
        kernel,
        out_shape=(
            pltpu.VMEM((8, TOK), F32),
            pltpu.VMEM((192, 384), BF16),
            pltpu.VMEM((384, 1024), F32),
        ),
        in_specs=[hbm] * 5,
        out_specs=(vmem, vmem, vmem),
        scratch_shapes=[
            pltpu.VMEM((8, TOK), I32),
            pltpu.VMEM((8, TOK), BF16),
            pltpu.VMEM((TOK, 4096), BF16),
            pltpu.VMEM((192, 384), BF16),
            pltpu.VMEM((384, 4096), BF16),
            pltpu.VMEM((NE * 16, 512), BF16),
            pltpu.VMEM((512, 512), BF16),
            pltpu.VMEM((4, NE * 16, LANE), BF16),
            pltpu.VMEM((4, NE * 16, LANE), BF16),
            pltpu.VMEM((4, NE * 16, LANE), BF16),
            pltpu.VMEM((NE, 1, 512), F32),
            pltpu.VMEM((NE, 1, 512), F32),
            pltpu.VMEM((ROWS, LANE), F32),
            pltpu.VMEM((ROWS, 4096), BF16),
            pltpu.VMEM((GROUPS, 4, ROWS, 512), BF16),
            pltpu.VMEM((GROUPS, 4, ROWS, 512), BF16),
            pltpu.VMEM((GROUPS, 3, ROWS, 512), BF16),
            pltpu.VMEM((GROUPS, 3, ROWS, 512), BF16),
            pltpu.VMEM((3, 192, 384), BF16),
            pltpu.VMEM((NE, 1, 512), F32),
            pltpu.VMEM((2, NE, 1, 512), F32),
            pltpu.VMEM((CAP, NE, LANE), F32),
            pltpu.VMEM((8, TOK), F32),
            pltpu.VMEM((8, TOK), F32),
            dma, dma((4,)), dma, dma((18,)), dma((12,)), dma((3,)), dma, dma((3,)), dma((3,)), dma((3,)), dma, dma,
        ],
        compiler_params=pltpu.CompilerParams(
            collective_id=0, has_side_effects=True, vmem_limit_bytes=60 * 1024 * 1024
        ),
        name="exchange",
    )(expert_ids.T, gate_values.T, grad_out, saved_hidden[0, 0], down_weight[0])
    gg, hg, dw = pl.pallas_call(
        flush,
        out_shape=(
            jax.ShapeDtypeStruct((8, TOK), F32),
            jax.ShapeDtypeStruct((192, 384), BF16),
            jax.ShapeDtypeStruct((384, 1024), F32),
        ),
        in_specs=[vmem] * 3,
        out_specs=(hbm,) * 3,
        scratch_shapes=[dma((3,))],
        compiler_params=pltpu.CompilerParams(vmem_limit_bytes=1024 * 1024),
        name="flush",
    )(gg, hg, dw)
    return (gg.T, hg[None, None], dw[None])


def solution(mesh):
    return jax.shard_map(
        on_device,
        mesh=mesh,
        in_specs=(
            P(("dp", "expert"), None),
            P(("dp", "expert"), None),
            P(("dp", "expert"), None),
            P("dp", "expert", None, "tensor"),
            P("expert", "tensor", None),
        ),
        out_specs=(
            P(("dp", "expert"), None),
            P("dp", "expert", None, "tensor"),
            P("expert", "tensor", "dp"),
        ),
        check_vma=False,
    )
```

```python
import jax
import jax.numpy as jnp
from jax import lax
from jax.experimental import pallas as pl
from jax.experimental.pallas import tpu as pltpu
from jax.sharding import PartitionSpec as P

CAP = 4
NZ = 12
NLO = 4
NX = 4
NT = 4
NE = NZ * NLO
GROUPS = 3
PER = NE // GROUPS
ROWS = PER * CAP
TOK = 128
LANE = 128
F32 = jnp.float32
BF16 = jnp.bfloat16
I32 = jnp.int32
MESH = pl.DeviceIdType.MESH


def offset_of(position):
    p = (position + 8) % NZ
    odd = p % 2
    return 6 + (1 - odd) * (p // 2) - odd * ((p + 1) // 2)


def iota(shape, dim):
    return lax.broadcasted_iota(I32, shape, dim)


def dot(a, b, dims=((1,), (0,))):
    return lax.dot_general(a, b, (dims, ((), ())), preferred_element_type=F32)


def crosses(a, b):
    square = (b - a) * (b - a)
    return square // 9 + ((square // 4) % 2) * ((a * (3 - a)) // 2)


def kernel(ids_in, gates_in, grad_in, hidden_in, weight_ref,
           gg_ref, hg_ref, dw_ref,
           ids_ref, gates_ref, grad_ref, hidden_ref, w_buf, pick_buf, g_buf, out_buf, in_buf, in2_buf,
           gout_buf, gin_buf, gate_buf, x_buf, xw_buf, xw2_buf, bw_buf, bw2_buf, h_buf,
           tout_buf, tin_buf, tsel_buf, part_buf, parts_buf,
           w_sem, load_sem, share_sem, send_sem, a_sem, g_sem, h_sem, p1_sem, b_sem, p2_sem, t_sem, d_sem):
    x = lax.axis_index("dp")
    e = lax.axis_index("expert")
    t = lax.axis_index("tensor")
    z, lo = e // NLO, e % NLO
    hi, core = t // 2, t % 2

    def at_offset(dz, lo2, far):
        return {"dp": x, "expert": ((z + dz) % NZ) * NLO + lo2, "tensor": ((hi + far) % 2) * 2 + core}

    def x_peer(r):
        return {"dp": (x + r) % NX, "expert": e, "tensor": t}

    def t_peer(r):
        return {"dp": x, "expert": e, "tensor": (t + r) % NT}

    partner = {"dp": x, "expert": e, "tensor": hi * 2 + (1 - core)}

    loads = [pltpu.make_async_copy(a, b, load_sem.at[i]) for i, (a, b) in enumerate(
        [(ids_in, ids_ref), (gates_in, gates_ref), (grad_in, grad_ref), (hidden_in, hidden_ref)])]
    for load in loads:
        load.start()
    for half in range(2):
        for q in range(4):
            at = pl.multiple_of(q * 1024 + ((core + half) % 2) * 512, 512)
            pltpu.make_async_copy(
                weight_ref.at[:, pl.ds(at, 512)], w_buf.at[half, :, pl.ds(q * 512, 512)], w_sem).start()

    barrier = pltpu.get_barrier_semaphore()

    def greet_at(dz, lo2, hi2):
        pl.semaphore_signal(barrier, inc=1, device_id_type=MESH, device_id={
            "dp": x, "expert": ((z + dz) % NZ) * NLO + lo2, "tensor": hi2 * 2 + core})

    def greet(dz, carry):
        for lo2 in range(NLO):
            for hi2 in range(2):
                greet_at(dz, lo2, hi2)
        return carry

    lax.fori_loop(1, NZ, greet, 0)
    for r in range(1, 4):
        for hi2 in range(2):
            greet_at(0, (lo + r) % NLO, hi2)
    greet_at(0, lo, 1 - hi)
    pl.semaphore_signal(barrier, inc=1, device_id=partner, device_id_type=MESH)
    for r in range(1, 4):
        pl.semaphore_signal(barrier, inc=1, device_id=x_peer(r), device_id_type=MESH)

    row = iota((NE, TOK), 0)
    where_z = z + offset_of(row // NLO)
    expert = (where_z % NZ) * NLO + row % NLO
    member = jnp.zeros((NE, TOK), F32)
    gate = jnp.zeros((NE, TOK), F32)
    loads[0].wait()
    loads[1].wait()
    gate_rows = gates_ref[...].astype(F32)
    for k in range(8):
        hit = ids_ref[k:k + 1, :] == expert
        member = member + hit.astype(F32)
        gate = gate + jnp.where(hit, gate_rows[k:k + 1, :], 0.0)
    earlier = (iota((TOK, TOK), 0) < iota((TOK, TOK), 1)).astype(F32).astype(BF16)
    before = dot(member.astype(BF16), earlier)
    code = jnp.where((member > 0) & (before < CAP), before, -1.0)
    lane = iota((NE, LANE), 1)
    sent_gates = jnp.zeros((NE, LANE), F32)
    for c in range(CAP):
        picked = jnp.sum(jnp.where(code == c, gate, 0.0), axis=1, keepdims=True)
        sent_gates = jnp.where(lane == c, picked, sent_gates)
    for s in range(NE):
        gout_buf[s] = sent_gates[s:s + 1, :]

    spread = (iota((NE * 16, NE), 0) // 16 == iota((NE * 16, NE), 1)).astype(F32).astype(BF16)
    code_wide = dot(spread, code.astype(BF16))
    place = iota((NE * 16, TOK), 0)
    chosen = code_wide == (place % CAP).astype(F32)
    part = (place // CAP) % 4
    for d in range(4):
        pick_buf[:, d * TOK:(d + 1) * TOK] = jnp.where(chosen & (part == d), 1.0, 0.0).astype(BF16)
    loads[2].wait()
    for q in range(4):
        for d in range(4):
            at = pl.multiple_of(q * 1024 + core * 512 + d * LANE, LANE)
            g_buf[d * TOK:(d + 1) * TOK, q * LANE:(q + 1) * LANE] = grad_ref[:, pl.ds(at, LANE)]
    for m in range(GROUPS):
        made = dot(pick_buf[m * 256:(m + 1) * 256, :], g_buf[...]).astype(BF16)
        for q in range(4):
            out_buf[q, m * 256:(m + 1) * 256, :] = made[:, q * LANE:(q + 1) * LANE]

    pl.semaphore_wait(barrier, 95 + 4)

    def block(ref, s, planes=slice(None)):
        return ref.at[planes, pl.ds(pl.multiple_of(s * 16, 16), 16), :]

    def send_rows(p, lo2, m):
        far = crosses(lo, lo2)
        device = at_offset(offset_of(p), lo2, far)
        planes = pl.ds(((hi + far) % 2) * 2, 2) if m == 1 else slice(None)
        rows_sem = a_sem.at[p] if m == 2 else a_sem.at[m]
        pltpu.make_async_remote_copy(
            src_ref=gout_buf.at[p * NLO + lo2], dst_ref=gin_buf.at[p * NLO + lo],
            send_sem=send_sem.at[1], recv_sem=g_sem.at[m], device_id=device, device_id_type=MESH).start()
        pltpu.make_async_remote_copy(
            src_ref=block(out_buf, p * NLO + lo2, planes), dst_ref=block(in_buf, p * NLO + lo, planes),
            send_sem=send_sem.at[0 if m == 1 else 14], recv_sem=rows_sem, device_id=device,
            device_id_type=MESH).start()

    def send_group(m):
        def body(p, carry):
            for lo2 in range(NLO):
                send_rows(p, lo2, m)
            return carry
        return body

    mine = 3 * NLO + lo
    lax.fori_loop(4, 8, send_group(1), 0)
    for r in range(1, 4):
        send_rows(3, (lo + r) % NLO, 0)
    lax.fori_loop(0, 3, send_group(0), 0)
    pltpu.make_async_copy(block(out_buf, mine), block(in_buf, mine), a_sem.at[0]).start()
    pltpu.make_async_copy(gout_buf.at[mine], gin_buf.at[mine], g_sem.at[0]).start()
    for r in range(1, 4):
        pltpu.make_async_remote_copy(
            src_ref=hidden_in, dst_ref=h_buf.at[r - 1],
            send_sem=send_sem.at[2], recv_sem=h_sem, device_id=x_peer(r), device_id_type=MESH).start()
    for p in range(8, 12):
        for lo2 in range(NLO):
            send_rows(p, lo2, 2)

    turn_row, turn_col = iota((256, 256), 0), iota((256, 256), 1)
    turn = ((turn_row // 64 == (turn_col // 4) % 4)
            & ((turn_row // 4) % 16 == turn_col // 16)
            & (turn_row % 4 == turn_col % 4)).astype(F32).astype(BF16)

    def natural(ref, m, xw):
        rows = jnp.concatenate([ref[q, m * 256:(m + 1) * 256, :] for q in range(4)], axis=1)
        turned = dot(turn, rows).astype(BF16)
        scale = gate_buf[...]
        for q in range(4):
            for d in range(4):
                piece = turned[d * ROWS:(d + 1) * ROWS, q * LANE:(q + 1) * LANE]
                at = q * 512 + d * LANE
                x_buf[:, at:at + LANE] = piece
                xw[m, q, :, d * LANE:(d + 1) * LANE] = (piece.astype(F32) * scale).astype(BF16)

    def wait_bytes(ref, sem):
        pltpu.make_async_copy(ref, ref, sem).wait()

    own_lane = iota((ROWS, LANE), 1) == iota((ROWS, LANE), 0) % CAP

    def core_copy(m, rows):
        return pltpu.make_async_remote_copy(
            src_ref=in_buf.at[:, rows, :], dst_ref=in2_buf.at[:, rows, :],
            send_sem=send_sem.at[3 + m], recv_sem=p1_sem.at[m], device_id=partner, device_id_type=MESH)

    def rows_of(m):
        return [pl.multiple_of(((z + NZ - offset_of(m * 4 + i)) % NZ) * 16, 16) for i in range(4)]

    def take_rows(m):
        rows = pl.ds(m * 256, 256)
        if m == 2:
            for p in range(8, 12):
                part_rows = pl.ds(p * 64, 64)
                wait_bytes(in_buf.at[:, part_rows, :], a_sem.at[p])
                core_copy(m, part_rows).start()
        elif m == 1:
            got, lacking = pl.ds(hi * 2, 2), pl.ds((1 - hi) * 2, 2)
            wait_bytes(in_buf.at[got, rows, :], a_sem.at[m])
            pltpu.make_async_remote_copy(
                src_ref=in_buf.at[got, rows, :], dst_ref=in_buf.at[got, rows, :],
                send_sem=send_sem.at[15], recv_sem=share_sem, device_id=t_peer(2), device_id_type=MESH).start()
            wait_bytes(in_buf.at[lacking, rows, :], share_sem)
            core_copy(m, rows).start()
        else:
            wait_bytes(in_buf.at[:, rows, :], a_sem.at[m])
            core_copy(m, rows).start()
        wait_bytes(gin_buf.at[pl.ds(m * PER, PER)], g_sem.at[m])
        for s in range(PER):
            for c in range(CAP):
                gate_buf[s * CAP + c:s * CAP + c + 1, :] = gin_buf[m * PER + s]
        column = jnp.sum(jnp.where(own_lane, gate_buf[...], 0.0), axis=1, keepdims=True)
        gate_buf[...] = jnp.broadcast_to(column, (ROWS, LANE))
        natural(in_buf, m, xw_buf)
        for r in range(1, 4):
            pltpu.make_async_remote_copy(
                src_ref=xw_buf.at[m, (x + r) % NX], dst_ref=bw_buf.at[m, r - 1],
                send_sem=send_sem.at[6 + m], recv_sem=b_sem.at[m], device_id=x_peer(r), device_id_type=MESH).start()
        return dot(x_buf[...], w_buf[0], ((1,), (1,)))

    def give_back(p, lo2, m):
        for hi2 in range(2):
            pltpu.make_async_remote_copy(
                src_ref=tout_buf.at[p * NLO + lo2], dst_ref=tin_buf.at[hi, p * NLO + lo],
                send_sem=send_sem.at[9 if hi2 == 0 else 16], recv_sem=t_sem.at[m], device_id_type=MESH, device_id={
                    "dp": x, "expert": ((z + NZ - offset_of(p)) % NZ) * NLO + lo2,
                    "tensor": hi2 * 2 + core}).start()

    def back_group(m):
        def body(p, carry):
            for lo2 in range(NLO):
                give_back(p, lo2, m)
            return carry
        return body

    def up_and_back(m, up_own):
        wait_bytes(in2_buf.at[:, pl.ds(m * 256, 256), :], p1_sem.at[m])
        natural(in2_buf, m, xw2_buf)
        up = up_own + dot(x_buf[...], w_buf[1], ((1,), (1,)))
        wide_gate = jnp.concatenate([gate_buf[...]] * 3, axis=1)
        grads = (wide_gate * up).astype(BF16)
        for i, at in enumerate(rows_of(m)):
            p = m * 4 + i
            rows16 = hidden_ref[pl.ds(at, 16), :]
            total = jnp.sum(rows16.astype(F32) * up[i * 16:(i + 1) * 16, :], axis=1, keepdims=True)
            wide = jnp.where(own_lane[:16], total, 0.0)
            for s in range(4):
                tout_buf[p * NLO + s] = jnp.sum(wide[s * 4:s * 4 + 4, :], axis=0, keepdims=True)
            hg_ref[pl.ds(at, 16), :] = grads[i * 16:(i + 1) * 16, :]
        if m == 0:
            for r in range(1, 4):
                give_back(3, (lo + r) % NLO, 0)
            pltpu.make_async_copy(tout_buf.at[mine], tin_buf.at[hi, mine], t_sem.at[0]).start()
            pltpu.make_async_remote_copy(
                src_ref=tout_buf.at[mine], dst_ref=tin_buf.at[hi, mine],
                send_sem=send_sem.at[17], recv_sem=t_sem.at[0], device_id=t_peer(2), device_id_type=MESH).start()
        lax.fori_loop(m * 4, m * 4 + (3 if m == 0 else 4), back_group(m), 0)

    def pass_on(m):
        wait_bytes(bw_buf.at[m], b_sem.at[m])
        pltpu.make_async_remote_copy(
            src_ref=bw_buf.at[m], dst_ref=bw2_buf.at[m],
            send_sem=send_sem.at[10 + m], recv_sem=p2_sem.at[m], device_id=partner, device_id_type=MESH).start()

    def contract(m):
        at_rows = rows_of(m)
        held = jnp.concatenate(
            [hidden_ref[pl.ds(at, 16), :] for at in at_rows]
            + [h_buf[r, pl.ds(at, 16), :] for r in range(3) for at in at_rows], axis=0)
        first = jnp.concatenate([xw_buf[m, x]] + [bw_buf[m, r] for r in range(3)], axis=0)
        near = dot(held, first, ((0,), (0,)))
        lane0 = pl.ds(pl.multiple_of(core * 512, 512), 512)
        lane1 = pl.ds(pl.multiple_of((1 - core) * 512, 512), 512)
        dw_ref[:, lane0] = near if m == 0 else dw_ref[:, lane0] + near
        wait_bytes(bw2_buf.at[m], p2_sem.at[m])
        second = jnp.concatenate([xw2_buf[m, x]] + [bw2_buf[m, r] for r in range(3)], axis=0)
        far_half = dot(held, second, ((0,), (0,)))
        dw_ref[:, lane1] = far_half if m == 0 else dw_ref[:, lane1] + far_half

    loads[3].wait()
    wait_bytes(w_buf, w_sem)
    up_and_back(0, take_rows(0))
    pass_on(0)
    up_and_back(1, take_rows(1))
    wait_bytes(h_buf, h_sem)
    contract(0)
    pass_on(1)
    up_and_back(2, take_rows(2))
    contract(1)
    pass_on(2)
    contract(2)

    for m in range(GROUPS):
        wait_bytes(tin_buf.at[:, pl.ds(m * PER, PER)], t_sem.at[m])
        for s in range(m * PER, (m + 1) * PER):
            tsel_buf[s:s + 1, :] = tin_buf[0, s] + tin_buf[1, s]
    value = jnp.zeros((NE, TOK), F32)
    for c in range(CAP):
        column = jnp.sum(jnp.where(lane == c, tsel_buf[...], 0.0), axis=1, keepdims=True)
        value = jnp.where(code == c, column, value)
    for k in range(8):
        hit = ids_ref[k:k + 1, :] == expert
        part_buf[k:k + 1, :] = jnp.sum(jnp.where(hit, value, 0.0), axis=0, keepdims=True)
    last = pltpu.make_async_remote_copy(
        src_ref=part_buf, dst_ref=parts_buf,
        send_sem=send_sem.at[13], recv_sem=d_sem, device_id=partner, device_id_type=MESH)
    last.start()
    last.wait()
    gg_ref[...] = part_buf[...] + parts_buf[...]

    wait_bytes(out_buf.at[pl.ds(0, 2), pl.ds(0, 256), :], send_sem.at[0])
    wait_bytes(out_buf.at[:, pl.ds(0, 31 * 16), :], send_sem.at[14])
    wait_bytes(in_buf.at[pl.ds(0, 2), pl.ds(0, 256), :], send_sem.at[15])
    wait_bytes(gout_buf.at[pl.ds(0, 47)], send_sem.at[1])
    wait_bytes(h_buf, send_sem.at[2])
    for m in range(GROUPS):
        wait_bytes(in_buf.at[:, pl.ds(m * 256, 256), :], send_sem.at[3 + m])
        wait_bytes(bw_buf.at[m], send_sem.at[6 + m])
        wait_bytes(bw_buf.at[m], send_sem.at[10 + m])
    wait_bytes(tout_buf.at[pl.ds(0, 47)], send_sem.at[9])
    wait_bytes(tout_buf.at[pl.ds(0, 47)], send_sem.at[16])
    wait_bytes(tout_buf.at[0], send_sem.at[17])


def flush(gg_ref, hg_ref, dw_ref, gg_out, hg_out, dw_out, sem):
    moves = [pltpu.make_async_copy(a, b, sem.at[i]) for i, (a, b) in enumerate(
        [(dw_ref, dw_out), (hg_ref, hg_out), (gg_ref, gg_out)])]
    for move in moves:
        move.start()
    for move in moves:
        move.wait()


def on_device(grad_out, expert_ids, gate_values, saved_hidden, down_weight):
    vmem = pl.BlockSpec(memory_space=pltpu.VMEM)
    hbm = pl.BlockSpec(memory_space=pltpu.HBM)
    dma = pltpu.SemaphoreType.DMA
    gg, hg, dw = pl.pallas_call(
        kernel,
        out_shape=(
            pltpu.VMEM((8, TOK), F32),
            pltpu.VMEM((192, 384), BF16),
            pltpu.VMEM((384, 1024), F32),
        ),
        in_specs=[hbm] * 5,
        out_specs=(vmem, vmem, vmem),
        scratch_shapes=[
            pltpu.VMEM((8, TOK), I32),
            pltpu.VMEM((8, TOK), BF16),
            pltpu.VMEM((TOK, 4096), BF16),
            pltpu.VMEM((192, 384), BF16),
            pltpu.VMEM((2, 384, 2048), BF16),
            pltpu.VMEM((NE * 16, 512), BF16),
            pltpu.VMEM((512, 512), BF16),
            pltpu.VMEM((4, NE * 16, LANE), BF16),
            pltpu.VMEM((4, NE * 16, LANE), BF16),
            pltpu.VMEM((4, NE * 16, LANE), BF16),
            pltpu.VMEM((NE, 1, LANE), F32),
            pltpu.VMEM((NE, 1, LANE), F32),
            pltpu.VMEM((ROWS, LANE), F32),
            pltpu.VMEM((ROWS, 2048), BF16),
            pltpu.VMEM((GROUPS, 4, ROWS, 512), BF16),
            pltpu.VMEM((GROUPS, 4, ROWS, 512), BF16),
            pltpu.VMEM((GROUPS, 3, ROWS, 512), BF16),
            pltpu.VMEM((GROUPS, 3, ROWS, 512), BF16),
            pltpu.VMEM((3, 192, 384), BF16),
            pltpu.VMEM((NE, 1, LANE), F32),
            pltpu.VMEM((2, NE, 1, LANE), F32),
            pltpu.VMEM((NE, LANE), F32),
            pltpu.VMEM((8, TOK), F32),
            pltpu.VMEM((8, TOK), F32),
            dma, dma((4,)), dma, dma((18,)), dma((12,)), dma((3,)), dma, dma((3,)), dma((3,)), dma((3,)), dma((3,)), dma,
        ],
        compiler_params=pltpu.CompilerParams(
            collective_id=0, has_side_effects=True, vmem_limit_bytes=60 * 1024 * 1024
        ),
        name="exchange",
    )(expert_ids.T, gate_values.T, grad_out, saved_hidden[0, 0], down_weight[0])
    gg, hg, dw = pl.pallas_call(
        flush,
        out_shape=(
            jax.ShapeDtypeStruct((8, TOK), F32),
            jax.ShapeDtypeStruct((192, 384), BF16),
            jax.ShapeDtypeStruct((384, 1024), F32),
        ),
        in_specs=[vmem] * 3,
        out_specs=(hbm,) * 3,
        scratch_shapes=[dma((3,))],
        compiler_params=pltpu.CompilerParams(vmem_limit_bytes=1024 * 1024),
        name="flush",
    )(gg, hg, dw)
    return (gg.T, hg[None, None], dw[None])


def solution(mesh):
    return jax.shard_map(
        on_device,
        mesh=mesh,
        in_specs=(
            P(("dp", "expert"), None),
            P(("dp", "expert"), None),
            P(("dp", "expert"), None),
            P("dp", "expert", None, "tensor"),
            P("expert", "tensor", None),
        ),
        out_specs=(
            P(("dp", "expert"), None),
            P("dp", "expert", None, "tensor"),
            P("expert", "tensor", "dp"),
        ),
        check_vma=False,
    )
```

```python
import jax
import jax.numpy as jnp
from jax import lax
from jax.experimental import pallas as pl
from jax.experimental.pallas import tpu as pltpu
from jax.sharding import PartitionSpec as P

CAP = 4
NZ = 12
NLO = 4
NX = 4
NT = 4
NE = NZ * NLO
GROUPS = 3
PER = NE // GROUPS
ROWS = PER * CAP
TOK = 128
LANE = 128
F32 = jnp.float32
BF16 = jnp.bfloat16
I32 = jnp.int32
MESH = pl.DeviceIdType.MESH


def offset_of(position):
    p = (position + 8) % NZ
    odd = p % 2
    return 6 + (1 - odd) * (p // 2) - odd * ((p + 1) // 2)


def iota(shape, dim):
    return lax.broadcasted_iota(I32, shape, dim)


def dot(a, b, dims=((1,), (0,))):
    return lax.dot_general(a, b, (dims, ((), ())), preferred_element_type=F32)


def crosses(a, b):
    square = (b - a) * (b - a)
    return square // 9 + ((square // 4) % 2) * ((a * (3 - a)) // 2)


def kernel(ids_in, gates_in, grad_in, hidden_in, weight_ref,
           gg_ref, hg_ref, dw_ref,
           ids_ref, gates_ref, grad_ref, hidden_ref, w_buf, pick_buf, g_buf, out_buf, in_buf, in2_buf,
           gout_buf, gin_buf, gate_buf, x_buf, xw_buf, xw2_buf, bw_buf, bw2_buf, h_buf,
           tout_buf, tin_buf, tsel_buf, part_buf, parts_buf,
           w_sem, load_sem, share_sem, send_sem, a_sem, g_sem, h_sem, p1_sem, b_sem, p2_sem, t_sem, d_sem):
    x = lax.axis_index("dp")
    e = lax.axis_index("expert")
    t = lax.axis_index("tensor")
    z, lo = e // NLO, e % NLO
    hi, core = t // 2, t % 2

    def at_offset(dz, lo2, far):
        return {"dp": x, "expert": ((z + dz) % NZ) * NLO + lo2, "tensor": ((hi + far) % 2) * 2 + core}

    def x_peer(r):
        return {"dp": (x + r) % NX, "expert": e, "tensor": t}

    def t_peer(r):
        return {"dp": x, "expert": e, "tensor": (t + r) % NT}

    partner = {"dp": x, "expert": e, "tensor": hi * 2 + (1 - core)}

    loads = [pltpu.make_async_copy(a, b, load_sem.at[i]) for i, (a, b) in enumerate(
        [(ids_in, ids_ref), (gates_in, gates_ref), (grad_in, grad_ref), (hidden_in, hidden_ref)])]
    for load in loads:
        load.start()
    for half in range(2):
        for q in range(4):
            at = pl.multiple_of(q * 1024 + ((core + half) % 2) * 512, 512)
            pltpu.make_async_copy(
                weight_ref.at[:, pl.ds(at, 512)], w_buf.at[half, :, pl.ds(q * 512, 512)], w_sem).start()

    barrier = pltpu.get_barrier_semaphore()

    def greet_at(dz, lo2, hi2):
        pl.semaphore_signal(barrier, inc=1, device_id_type=MESH, device_id={
            "dp": x, "expert": ((z + dz) % NZ) * NLO + lo2, "tensor": hi2 * 2 + core})

    def greet(dz, carry):
        for lo2 in range(NLO):
            for hi2 in range(2):
                greet_at(dz, lo2, hi2)
        return carry

    lax.fori_loop(1, NZ, greet, 0)
    for r in range(1, 4):
        for hi2 in range(2):
            greet_at(0, (lo + r) % NLO, hi2)
    greet_at(0, lo, 1 - hi)
    pl.semaphore_signal(barrier, inc=1, device_id=partner, device_id_type=MESH)
    for r in range(1, 4):
        pl.semaphore_signal(barrier, inc=1, device_id=x_peer(r), device_id_type=MESH)

    row = iota((NE, TOK), 0)
    where_z = z + offset_of(row // NLO)
    expert = (where_z % NZ) * NLO + row % NLO
    member = jnp.zeros((NE, TOK), F32)
    gate = jnp.zeros((NE, TOK), F32)
    loads[0].wait()
    loads[1].wait()
    gate_rows = gates_ref[...].astype(F32)
    for k in range(8):
        hit = ids_ref[k:k + 1, :] == expert
        member = member + hit.astype(F32)
        gate = gate + jnp.where(hit, gate_rows[k:k + 1, :], 0.0)
    earlier = (iota((TOK, TOK), 0) < iota((TOK, TOK), 1)).astype(F32).astype(BF16)
    before = dot(member.astype(BF16), earlier)
    code = jnp.where((member > 0) & (before < CAP), before, -1.0)
    lane = iota((NE, LANE), 1)
    sent_gates = jnp.zeros((NE, LANE), F32)
    for c in range(CAP):
        picked = jnp.sum(jnp.where(code == c, gate, 0.0), axis=1, keepdims=True)
        sent_gates = jnp.where(lane == c, picked, sent_gates)
    for s in range(NE):
        gout_buf[s] = sent_gates[s:s + 1, :]

    spread = (iota((NE * 16, NE), 0) // 16 == iota((NE * 16, NE), 1)).astype(F32).astype(BF16)
    code_wide = dot(spread, code.astype(BF16))
    place = iota((NE * 16, TOK), 0)
    chosen = code_wide == (place % CAP).astype(F32)
    part = (place // CAP) % 4
    for d in range(4):
        pick_buf[:, d * TOK:(d + 1) * TOK] = jnp.where(chosen & (part == d), 1.0, 0.0).astype(BF16)
    loads[2].wait()
    for q in range(4):
        for d in range(4):
            at = pl.multiple_of(q * 1024 + core * 512 + d * LANE, LANE)
            g_buf[d * TOK:(d + 1) * TOK, q * LANE:(q + 1) * LANE] = grad_ref[:, pl.ds(at, LANE)]
    for m in range(GROUPS):
        made = dot(pick_buf[m * 256:(m + 1) * 256, :], g_buf[...]).astype(BF16)
        for q in range(4):
            out_buf[q, m * 256:(m + 1) * 256, :] = made[:, q * LANE:(q + 1) * LANE]

    pl.semaphore_wait(barrier, 95 + 4)

    def block(ref, s, planes=slice(None)):
        return ref.at[planes, pl.ds(pl.multiple_of(s * 16, 16), 16), :]

    def send_rows(p, lo2, m):
        far = crosses(lo, lo2)
        device = at_offset(offset_of(p), lo2, far)
        planes = pl.ds(((hi + far) % 2) * 2, 2) if m == 1 else slice(None)
        rows_sem = a_sem.at[p] if m == 2 else a_sem.at[m]
        pltpu.make_async_remote_copy(
            src_ref=gout_buf.at[p * NLO + lo2], dst_ref=gin_buf.at[p * NLO + lo],
            send_sem=send_sem.at[1], recv_sem=g_sem.at[m], device_id=device, device_id_type=MESH).start()
        pltpu.make_async_remote_copy(
            src_ref=block(out_buf, p * NLO + lo2, planes), dst_ref=block(in_buf, p * NLO + lo, planes),
            send_sem=send_sem.at[0 if m == 1 else 14], recv_sem=rows_sem, device_id=device,
            device_id_type=MESH).start()

    def send_group(m):
        def body(p, carry):
            for lo2 in range(NLO):
                send_rows(p, lo2, m)
            return carry
        return body

    mine = 3 * NLO + lo
    lax.fori_loop(4, 8, send_group(1), 0)
    for r in range(1, 4):
        send_rows(3, (lo + r) % NLO, 0)
    lax.fori_loop(0, 3, send_group(0), 0)
    pltpu.make_async_copy(block(out_buf, mine), block(in_buf, mine), a_sem.at[0]).start()
    pltpu.make_async_copy(gout_buf.at[mine], gin_buf.at[mine], g_sem.at[0]).start()
    for r in range(1, 4):
        pltpu.make_async_remote_copy(
            src_ref=hidden_in, dst_ref=h_buf.at[r - 1],
            send_sem=send_sem.at[2], recv_sem=h_sem, device_id=x_peer(r), device_id_type=MESH).start()
    for lo2 in range(NLO):
        for p in range(8, 12):
            send_rows(p, lo2, 2)

    turn_row, turn_col = iota((256, 256), 0), iota((256, 256), 1)
    turn = ((turn_row // 64 == (turn_col // 4) % 4)
            & ((turn_row // 4) % 16 == turn_col // 16)
            & (turn_row % 4 == turn_col % 4)).astype(F32).astype(BF16)

    def natural(ref, m, xw):
        rows = jnp.concatenate([ref[q, m * 256:(m + 1) * 256, :] for q in range(4)], axis=1)
        turned = dot(turn, rows).astype(BF16)
        scale = gate_buf[...]
        for q in range(4):
            for d in range(4):
                piece = turned[d * ROWS:(d + 1) * ROWS, q * LANE:(q + 1) * LANE]
                at = q * 512 + d * LANE
                x_buf[:, at:at + LANE] = piece
                xw[m, q, :, d * LANE:(d + 1) * LANE] = (piece.astype(F32) * scale).astype(BF16)

    def wait_bytes(ref, sem):
        pltpu.make_async_copy(ref, ref, sem).wait()

    own_lane = iota((ROWS, LANE), 1) == iota((ROWS, LANE), 0) % CAP

    def core_copy(m, rows):
        return pltpu.make_async_remote_copy(
            src_ref=in_buf.at[:, rows, :], dst_ref=in2_buf.at[:, rows, :],
            send_sem=send_sem.at[3 + m], recv_sem=p1_sem.at[m], device_id=partner, device_id_type=MESH)

    def rows_of(m):
        return [pl.multiple_of(((z + NZ - offset_of(m * 4 + i)) % NZ) * 16, 16) for i in range(4)]

    def take_rows(m):
        rows = pl.ds(m * 256, 256)
        if m == 2:
            for p in range(8, 12):
                part_rows = pl.ds(p * 64, 64)
                wait_bytes(in_buf.at[:, part_rows, :], a_sem.at[p])
                core_copy(m, part_rows).start()
        elif m == 1:
            got, lacking = pl.ds(hi * 2, 2), pl.ds((1 - hi) * 2, 2)
            wait_bytes(in_buf.at[got, rows, :], a_sem.at[m])
            pltpu.make_async_remote_copy(
                src_ref=in_buf.at[got, rows, :], dst_ref=in_buf.at[got, rows, :],
                send_sem=send_sem.at[15], recv_sem=share_sem, device_id=t_peer(2), device_id_type=MESH).start()
            wait_bytes(in_buf.at[lacking, rows, :], share_sem)
            core_copy(m, rows).start()
        else:
            wait_bytes(in_buf.at[:, rows, :], a_sem.at[m])
            core_copy(m, rows).start()
        wait_bytes(gin_buf.at[pl.ds(m * PER, PER)], g_sem.at[m])
        for s in range(PER):
            for c in range(CAP):
                gate_buf[s * CAP + c:s * CAP + c + 1, :] = gin_buf[m * PER + s]
        column = jnp.sum(jnp.where(own_lane, gate_buf[...], 0.0), axis=1, keepdims=True)
        gate_buf[...] = jnp.broadcast_to(column, (ROWS, LANE))
        natural(in_buf, m, xw_buf)
        for r in range(1, 4):
            pltpu.make_async_remote_copy(
                src_ref=xw_buf.at[m, (x + r) % NX], dst_ref=bw_buf.at[m, r - 1],
                send_sem=send_sem.at[6 + m], recv_sem=b_sem.at[m], device_id=x_peer(r), device_id_type=MESH).start()
        return dot(x_buf[...], w_buf[0], ((1,), (1,)))

    def give_back(p, lo2, m):
        for hi2 in range(2):
            pltpu.make_async_remote_copy(
                src_ref=tout_buf.at[p * NLO + lo2], dst_ref=tin_buf.at[hi, p * NLO + lo],
                send_sem=send_sem.at[9 if hi2 == 0 else 16], recv_sem=t_sem.at[m], device_id_type=MESH, device_id={
                    "dp": x, "expert": ((z + NZ - offset_of(p)) % NZ) * NLO + lo2,
                    "tensor": hi2 * 2 + core}).start()

    def back_group(m):
        def body(p, carry):
            for lo2 in range(NLO):
                give_back(p, lo2, m)
            return carry
        return body

    def up_and_back(m, up_own):
        wait_bytes(in2_buf.at[:, pl.ds(m * 256, 256), :], p1_sem.at[m])
        natural(in2_buf, m, xw2_buf)
        up = up_own + dot(x_buf[...], w_buf[1], ((1,), (1,)))
        wide_gate = jnp.concatenate([gate_buf[...]] * 3, axis=1)
        grads = (wide_gate * up).astype(BF16)
        for i, at in enumerate(rows_of(m)):
            p = m * 4 + i
            rows16 = hidden_ref[pl.ds(at, 16), :]
            total = jnp.sum(rows16.astype(F32) * up[i * 16:(i + 1) * 16, :], axis=1, keepdims=True)
            wide = jnp.where(own_lane[:16], total, 0.0)
            for s in range(4):
                tout_buf[p * NLO + s] = jnp.sum(wide[s * 4:s * 4 + 4, :], axis=0, keepdims=True)
            hg_ref[pl.ds(at, 16), :] = grads[i * 16:(i + 1) * 16, :]
        if m == 0:
            for r in range(1, 4):
                give_back(3, (lo + r) % NLO, 0)
            pltpu.make_async_copy(tout_buf.at[mine], tin_buf.at[hi, mine], t_sem.at[0]).start()
            pltpu.make_async_remote_copy(
                src_ref=tout_buf.at[mine], dst_ref=tin_buf.at[hi, mine],
                send_sem=send_sem.at[17], recv_sem=t_sem.at[0], device_id=t_peer(2), device_id_type=MESH).start()
        lax.fori_loop(m * 4, m * 4 + (3 if m == 0 else 4), back_group(m), 0)

    def pass_on(m):
        wait_bytes(bw_buf.at[m], b_sem.at[m])
        pltpu.make_async_remote_copy(
            src_ref=bw_buf.at[m], dst_ref=bw2_buf.at[m],
            send_sem=send_sem.at[10 + m], recv_sem=p2_sem.at[m], device_id=partner, device_id_type=MESH).start()

    def contract(m):
        at_rows = rows_of(m)
        held = jnp.concatenate(
            [hidden_ref[pl.ds(at, 16), :] for at in at_rows]
            + [h_buf[r, pl.ds(at, 16), :] for r in range(3) for at in at_rows], axis=0)
        first = jnp.concatenate([xw_buf[m, x]] + [bw_buf[m, r] for r in range(3)], axis=0)
        near = dot(held, first, ((0,), (0,)))
        lane0 = pl.ds(pl.multiple_of(core * 512, 512), 512)
        lane1 = pl.ds(pl.multiple_of((1 - core) * 512, 512), 512)
        dw_ref[:, lane0] = near if m == 0 else dw_ref[:, lane0] + near
        wait_bytes(bw2_buf.at[m], p2_sem.at[m])
        second = jnp.concatenate([xw2_buf[m, x]] + [bw2_buf[m, r] for r in range(3)], axis=0)
        far_half = dot(held, second, ((0,), (0,)))
        dw_ref[:, lane1] = far_half if m == 0 else dw_ref[:, lane1] + far_half

    loads[3].wait()
    wait_bytes(w_buf, w_sem)
    up_and_back(0, take_rows(0))
    pass_on(0)
    up_and_back(1, take_rows(1))
    up_own = take_rows(2)
    pass_on(1)
    up_and_back(2, up_own)
    wait_bytes(h_buf, h_sem)
    contract(0)
    contract(1)
    pass_on(2)
    contract(2)

    for m in range(GROUPS):
        wait_bytes(tin_buf.at[:, pl.ds(m * PER, PER)], t_sem.at[m])
        for s in range(m * PER, (m + 1) * PER):
            tsel_buf[s:s + 1, :] = tin_buf[0, s] + tin_buf[1, s]
    value = jnp.zeros((NE, TOK), F32)
    for c in range(CAP):
        column = jnp.sum(jnp.where(lane == c, tsel_buf[...], 0.0), axis=1, keepdims=True)
        value = jnp.where(code == c, column, value)
    for k in range(8):
        hit = ids_ref[k:k + 1, :] == expert
        part_buf[k:k + 1, :] = jnp.sum(jnp.where(hit, value, 0.0), axis=0, keepdims=True)
    last = pltpu.make_async_remote_copy(
        src_ref=part_buf, dst_ref=parts_buf,
        send_sem=send_sem.at[13], recv_sem=d_sem, device_id=partner, device_id_type=MESH)
    last.start()
    last.wait()
    gg_ref[...] = part_buf[...] + parts_buf[...]

    wait_bytes(out_buf.at[pl.ds(0, 2), pl.ds(0, 256), :], send_sem.at[0])
    wait_bytes(out_buf.at[:, pl.ds(0, 31 * 16), :], send_sem.at[14])
    wait_bytes(in_buf.at[pl.ds(0, 2), pl.ds(0, 256), :], send_sem.at[15])
    wait_bytes(gout_buf.at[pl.ds(0, 47)], send_sem.at[1])
    wait_bytes(h_buf, send_sem.at[2])
    for m in range(GROUPS):
        wait_bytes(in_buf.at[:, pl.ds(m * 256, 256), :], send_sem.at[3 + m])
        wait_bytes(bw_buf.at[m], send_sem.at[6 + m])
        wait_bytes(bw_buf.at[m], send_sem.at[10 + m])
    wait_bytes(tout_buf.at[pl.ds(0, 47)], send_sem.at[9])
    wait_bytes(tout_buf.at[pl.ds(0, 47)], send_sem.at[16])
    wait_bytes(tout_buf.at[0], send_sem.at[17])


def flush(gg_ref, hg_ref, dw_ref, gg_out, hg_out, dw_out, sem):
    moves = [pltpu.make_async_copy(a, b, sem.at[i]) for i, (a, b) in enumerate(
        [(dw_ref, dw_out), (hg_ref, hg_out), (gg_ref, gg_out)])]
    for move in moves:
        move.start()
    for move in moves:
        move.wait()


def on_device(grad_out, expert_ids, gate_values, saved_hidden, down_weight):
    vmem = pl.BlockSpec(memory_space=pltpu.VMEM)
    hbm = pl.BlockSpec(memory_space=pltpu.HBM)
    dma = pltpu.SemaphoreType.DMA
    gg, hg, dw = pl.pallas_call(
        kernel,
        out_shape=(
            pltpu.VMEM((8, TOK), F32),
            pltpu.VMEM((192, 384), BF16),
            pltpu.VMEM((384, 1024), F32),
        ),
        in_specs=[hbm] * 5,
        out_specs=(vmem, vmem, vmem),
        scratch_shapes=[
            pltpu.VMEM((8, TOK), I32),
            pltpu.VMEM((8, TOK), BF16),
            pltpu.VMEM((TOK, 4096), BF16),
            pltpu.VMEM((192, 384), BF16),
            pltpu.VMEM((2, 384, 2048), BF16),
            pltpu.VMEM((NE * 16, 512), BF16),
            pltpu.VMEM((512, 512), BF16),
            pltpu.VMEM((4, NE * 16, LANE), BF16),
            pltpu.VMEM((4, NE * 16, LANE), BF16),
            pltpu.VMEM((4, NE * 16, LANE), BF16),
            pltpu.VMEM((NE, 1, LANE), F32),
            pltpu.VMEM((NE, 1, LANE), F32),
            pltpu.VMEM((ROWS, LANE), F32),
            pltpu.VMEM((ROWS, 2048), BF16),
            pltpu.VMEM((GROUPS, 4, ROWS, 512), BF16),
            pltpu.VMEM((GROUPS, 4, ROWS, 512), BF16),
            pltpu.VMEM((GROUPS, 3, ROWS, 512), BF16),
            pltpu.VMEM((GROUPS, 3, ROWS, 512), BF16),
            pltpu.VMEM((3, 192, 384), BF16),
            pltpu.VMEM((NE, 1, LANE), F32),
            pltpu.VMEM((2, NE, 1, LANE), F32),
            pltpu.VMEM((NE, LANE), F32),
            pltpu.VMEM((8, TOK), F32),
            pltpu.VMEM((8, TOK), F32),
            dma, dma((4,)), dma, dma((18,)), dma((12,)), dma((3,)), dma, dma((3,)), dma((3,)), dma((3,)), dma((3,)), dma,
        ],
        compiler_params=pltpu.CompilerParams(
            collective_id=0, has_side_effects=True, vmem_limit_bytes=60 * 1024 * 1024
        ),
        name="exchange",
    )(expert_ids.T, gate_values.T, grad_out, saved_hidden[0, 0], down_weight[0])
    gg, hg, dw = pl.pallas_call(
        flush,
        out_shape=(
            jax.ShapeDtypeStruct((8, TOK), F32),
            jax.ShapeDtypeStruct((192, 384), BF16),
            jax.ShapeDtypeStruct((384, 1024), F32),
        ),
        in_specs=[vmem] * 3,
        out_specs=(hbm,) * 3,
        scratch_shapes=[dma((3,))],
        compiler_params=pltpu.CompilerParams(vmem_limit_bytes=1024 * 1024),
        name="flush",
    )(gg, hg, dw)
    return (gg.T, hg[None, None], dw[None])


def solution(mesh):
    return jax.shard_map(
        on_device,
        mesh=mesh,
        in_specs=(
            P(("dp", "expert"), None),
            P(("dp", "expert"), None),
            P(("dp", "expert"), None),
            P("dp", "expert", None, "tensor"),
            P("expert", "tensor", None),
        ),
        out_specs=(
            P(("dp", "expert"), None),
            P("dp", "expert", None, "tensor"),
            P("expert", "tensor", "dp"),
        ),
        check_vma=False,
    )
```
